128 devices in a mesh: fsdp: 32 (over x, y_lo, z), tensor: 4 (over y_hi, core).
Axes of the slice: x: 4, y: 4 (y_hi: 2, y_lo: 2; y = y_hi * 2 + y_lo), z: 4, core: 2. Of those that a mesh axis runs over, the one named last changes fastest.
Arguments:
- tokens: bfloat16 [24576, 5120], P('fsdp', 'tensor'), may hold values from -48 to 48
- live_rows: int32 [32], P('fsdp'), may hold values from 128 to 768, as said below
- first_row: int32 [24576], P('fsdp'), may hold values from 0 to 767, as said below
- w_query: bfloat16 [5120, 2560], P('fsdp', 'tensor'), may hold values from -1 to 1
- w_key: bfloat16 [5120, 512], P('fsdp', 'tensor'), may hold values from -1 to 1
- w_value: bfloat16 [5120, 512], P('fsdp', 'tensor'), may hold values from -0.078125 to 0.078125
- w_out: bfloat16 [2560, 5120], P('tensor', 'fsdp'), may hold values from -1 to 1
- query_gain: float32 [2560], P('tensor'), may hold values from 0.5 to 1.5
- key_gain: float32 [512], P('tensor'), may hold values from 0.5 to 1.5
- out_gain: float32 [5120], P('tensor'), may hold values from 0.5 to 1.5
Outputs:
- output: bfloat16 [24576, 5120], P('fsdp', 'tensor')
The draws below stay inside these ranges and needn't reach their ends.
Inputs may be any that keep to these rules, and one draw needn't show every extreme that they name: `live_rows`: each entry is a multiple of 128; the largest value is reached on some index of every draw. `first_row`: each row's value is never above its own local index and never below the first local index of its pack (384 rows); the last row of each block begins a document of one row.
All inputs are finite; a program needn't handle non-finite values.
Results may differ from the reference program's by a relative error of at most 0.009.
Values may be sent and summed in bfloat16 or wider, within the bound.
A program may use at most 128 MiB of HBM per device.

```python
import math
import jax
import jax.numpy as jnp
from jax import lax

D = 5120
HEADS = 20
KV_HEADS = 4
HEAD_DIM = 128
BLOCK = 128
CAP = 768
HALF = 384
TOKENS = 24576
N_FSDP = 32
N_TENSOR = 4


def draw_tokens(key, part):
    values = jnp.clip(jax.random.normal(jax.random.fold_in(key, 1), (TOKENS, D), jnp.float32), -6.0, 6.0)
    return values.astype(jnp.bfloat16)


def draw_live_rows(key, part):
    devices = TOKENS // CAP
    total_blocks = CAP // BLOCK
    index = jnp.arange(devices, dtype=jnp.int32)
    base = total_blocks - index * (total_blocks - 1) // max(devices - 1, 1)
    jitter = jax.random.randint(jax.random.fold_in(key, 3), (devices,), 0, 2, dtype=jnp.int32)
    blocks = jnp.where(index == 0, total_blocks, jnp.maximum(base - jitter, 1))
    return (blocks * BLOCK).astype(jnp.int32)


def draw_first_row(key, part):
    devices = TOKENS // CAP
    local = jnp.arange(CAP, dtype=jnp.int32)[None, :]
    marks = jax.random.randint(jax.random.fold_in(key, 4), (devices, CAP), 0, 200, dtype=jnp.int32) == 0
    cuts = jax.random.randint(jax.random.fold_in(key, 5), (devices, 2), 1, CAP // 2, dtype=jnp.int32)
    marks = marks | (local % (CAP // 2) == 0) | (local == cuts[:, :1]) | (local == cuts[:, 1:] + CAP // 2)
    marks = marks | (local == CAP - 1)
    starts = lax.cummax(jnp.where(marks, local, 0), axis=1)
    return starts.reshape(TOKENS).astype(jnp.int32)


def draw_w_query(key, part):
    scale = jnp.power(3.0, jnp.repeat(jnp.arange(HEADS, dtype=jnp.float32), HEAD_DIM) / (HEADS - 1))
    noise = jax.random.normal(jax.random.fold_in(key, 6), (D, HEADS * HEAD_DIM), jnp.float32) / math.sqrt(D)
    return jnp.clip(noise * scale[None, :], -1.0, 1.0).astype(jnp.bfloat16)


def draw_w_key(key, part):
    scale = jnp.power(3.0, jnp.repeat(jnp.arange(KV_HEADS, dtype=jnp.float32), HEAD_DIM) / (KV_HEADS - 1))
    noise = jax.random.normal(jax.random.fold_in(key, 7), (D, KV_HEADS * HEAD_DIM), jnp.float32) / math.sqrt(D)
    return jnp.clip(noise * scale[None, :], -1.0, 1.0).astype(jnp.bfloat16)


def draw_w_out(key, part):
    scale = jnp.power(3.0, jnp.arange(D, dtype=jnp.float32) / (D - 1))
    fan = math.sqrt(HEADS * HEAD_DIM)
    noise = jax.random.normal(jax.random.fold_in(key, 8), (HEADS * HEAD_DIM, D), jnp.float32)
    return jnp.clip(noise * scale[None, :] / fan, -1.0, 1.0).astype(jnp.bfloat16)


def draw_query_gain(key, part):
    return jax.random.uniform(jax.random.fold_in(key, 9), (HEADS * HEAD_DIM,), jnp.float32, 0.5, 1.5)


def draw_key_gain(key, part):
    return jax.random.uniform(jax.random.fold_in(key, 10), (KV_HEADS * HEAD_DIM,), jnp.float32, 0.5, 1.5)


def block_levels(stream_key, shape, cuts, least, top_value):
    factor_of = 1.0
    for position, shards_of in cuts:
        draws = jax.random.uniform(jax.random.fold_in(jax.random.fold_in(stream_key, 6), position), (shards_of,), jnp.float32, least / len(cuts), top_value / len(cuts))
        factor_of = factor_of * jnp.repeat(jnp.exp(draws), shape[position] // shards_of).reshape((-1,) + (1,) * (len(shape) - 1 - position))
    return factor_of


def centred(key, extent, spread, most, pieces=(), kind=jnp.bfloat16):
    array = spread * jax.random.normal(key, extent, jnp.float32)
    if pieces:
        array = array * block_levels(key, extent, pieces, -0.22, 0.18)
    return jnp.clip(array, -most, most).astype(kind)


def setup_inputs(seed: int = 0) -> dict:
    splits = jax.random.split(jax.random.key(seed), 11)
    return {
        "tokens": draw_tokens(jax.random.fold_in(splits[10], 71), 0),
        "live_rows": draw_live_rows(jax.random.fold_in(splits[10], 71), 0),
        "first_row": draw_first_row(jax.random.fold_in(splits[10], 71), 0),
        "w_query": draw_w_query(jax.random.fold_in(splits[10], 71), 0),
        "w_key": draw_w_key(jax.random.fold_in(splits[10], 71), 0),
        "w_value": centred(splits[5], (D, KV_HEADS * HEAD_DIM), D ** -0.5, 0.078125, ((0, 32), (1, 4))),
        "w_out": draw_w_out(jax.random.fold_in(splits[10], 71), 0),
        "query_gain": draw_query_gain(jax.random.fold_in(splits[10], 71), 0),
        "key_gain": draw_key_gain(jax.random.fold_in(splits[10], 71), 0),
        "out_gain": jnp.clip(0.5 + 1.0 * jax.random.uniform(splits[9], (D,), jnp.float32) ** block_levels(splits[9], (D,), ((0, 4),), -0.2, 0.2), 0.5, 1.5),
    }


EPS = 1e-06
ROPE_BASE = 500000.0

def rotate(field, positions):
    half_dim = field.shape[-1] // 2
    freqs = jnp.power(ROPE_BASE, -(jnp.arange(half_dim, dtype=jnp.float32) * 2.0 / field.shape[-1]))
    angle = positions[:, None] * freqs[None, :]
    cosine = jnp.cos(angle)[:, None, :]
    sine_part = jnp.sin(angle)[:, None, :]
    first = field[..., :half_dim]
    second = field[..., half_dim:]
    return jnp.concatenate([first * cosine - second * sine_part, second * cosine + first * sine_part], axis=-1)

def attend(queries, keys, values, starts, offset):
    row_count = queries.shape[0]
    kv_count = keys.shape[1]
    group_size = queries.shape[1] // kv_count
    grouped = queries.reshape(row_count, kv_count, group_size, HEAD_DIM).astype(jnp.float32)
    scores = jnp.einsum('qkgd,skd->kgqs', grouped, keys.astype(jnp.float32)) / math.sqrt(HEAD_DIM)
    local = jnp.arange(row_count, dtype=jnp.int32)
    allowed = (local[None, :] >= (starts - offset)[:, None]) & (local[None, :] <= local[:, None])
    scores = jnp.where(allowed[None, None], scores, jnp.float32(-1e+30))
    peak_value = lax.optimization_barrier(jnp.max(scores, axis=-1, keepdims=True))
    expo = jnp.exp(scores - peak_value)
    totals = lax.optimization_barrier(jnp.sum(expo, axis=-1, keepdims=True))
    probs = (expo / totals).astype(jnp.bfloat16)
    mixed = jnp.einsum('kgqs,skd->qkgd', probs.astype(jnp.float32), values.astype(jnp.float32))
    return mixed.reshape(row_count, -1).astype(jnp.bfloat16)

def reference(tokens, live_rows, first_row, w_query, w_key, w_value, w_out, query_gain, key_gain, out_gain):
    blocks = tokens.reshape(N_FSDP, CAP, D)
    offsets = first_row.reshape(N_FSDP, CAP)

    def layer(items):
        inputs, live_count, starts = items
        query = jnp.dot(inputs, w_query, preferred_element_type=jnp.float32)
        key = jnp.dot(inputs, w_key, preferred_element_type=jnp.float32)
        value = jnp.dot(inputs, w_value, preferred_element_type=jnp.float32).astype(jnp.bfloat16)
        query_normed = query * lax.rsqrt(lax.optimization_barrier(jnp.mean(query * query, axis=1, keepdims=True)) + EPS) * query_gain
        key_normed = key * lax.rsqrt(lax.optimization_barrier(jnp.mean(key * key, axis=1, keepdims=True)) + EPS) * key_gain
        row_ids = jnp.arange(CAP, dtype=jnp.int32)
        positions = (row_ids - starts).astype(jnp.float32)
        query_rot = rotate(query_normed.reshape(CAP, HEADS, HEAD_DIM), positions).astype(jnp.bfloat16)
        key_rot = rotate(key_normed.reshape(CAP, KV_HEADS, HEAD_DIM), positions).astype(jnp.bfloat16)
        value_heads = value.reshape(CAP, KV_HEADS, HEAD_DIM)
        packs = []
        for pack_index in range(2):
            lower = pack_index * HALF
            packs.append(attend(query_rot[lower:lower + HALF], key_rot[lower:lower + HALF], value_heads[lower:lower + HALF], starts[lower:lower + HALF], lower))
        attended = jnp.concatenate(packs, axis=0)
        width = HEADS * HEAD_DIM // N_TENSOR
        attn_out = jnp.zeros((CAP, D), jnp.float32)
        for group in range(N_TENSOR):
            partial_value = jnp.dot(attended[:, group * width:(group + 1) * width], w_out[group * width:(group + 1) * width], preferred_element_type=jnp.float32).astype(jnp.bfloat16)
            partial_value = lax.optimization_barrier(partial_value)
            attn_out = attn_out + partial_value.astype(jnp.float32)
        scale = lax.rsqrt(lax.optimization_barrier(jnp.mean(attn_out * attn_out, axis=1, keepdims=True)) + EPS)
        result = (inputs.astype(jnp.float32) + attn_out * scale * out_gain).astype(jnp.bfloat16)
        return jnp.where((row_ids < live_count)[:, None], result, jnp.zeros_like(result))
    outputs = lax.map(layer, (blocks, live_rows, offsets))
    return outputs.reshape(TOKENS, D)
```

```python
import functools
import math

import jax
import jax.numpy as jnp
from jax import lax
from jax.experimental import pallas as pl
from jax.experimental.pallas import tpu as pltpu
from jax.sharding import PartitionSpec as P

D = 5120
HEADS = 20
KV_HEADS = 4
HEAD_DIM = 128
CAP = 768
HALF = 384
EPS = 1e-06
ROPE_BASE = 500000.0
SHARD = 160
QKV = 896
QW = 640
TCOL = 1280
MESH = pl.DeviceIdType.MESH

TOK_CHUNK = 64
TOK_N = CAP // TOK_CHUNK
ATT_CHUNK = 128
ATT_N = CAP // ATT_CHUNK

AG_SEMS = 1 + 2 * 22
SEM_W = 0
SEM_O = SEM_W + AG_SEMS
SEM_T = SEM_O + AG_SEMS
SEM_A = SEM_T + 4 * TOK_N
SEM_S = SEM_A + 4 * ATT_N
SEM_P = SEM_S + 6
SEM_N = SEM_P + 1


def kernel(
    tok_hbm,
    wq_hbm,
    wk_hbm,
    wv_hbm,
    wot_hbm,
    cos_ref,
    sin_ref,
    start_ref,
    gain_ref,
    ogain_ref,
    live_ref,
    out_hbm,
    wbuf,
    obuf,
    xall,
    xstage,
    acc,
    rot,
    vbuf,
    att,
    astage,
    oacc,
    res,
    sqt,
    sqr,
    send_sem,
    recv_sem,
    local_sem,
):
    f = lax.axis_index("fsdp")
    t = lax.axis_index("tensor")
    x, yl, z = f // 8, (f // 4) % 2, f % 4
    yh, core = t // 2, t % 2
    y = 2 * yh + yl

    def dev(dx=0, dy=0, dz=0, flip=0):
        ny = (y + dy) % 4
        nf = ((x + dx) % 4) * 8 + (ny % 2) * 4 + (z + dz) % 4
        nc = (core + flip) % 2
        return (nf, (ny // 2) * 2 + nc)

    ypair = ((x * 8 + (1 - yl) * 4 + z), t)
    swap_f = t * 8 + yl * 4 + z
    swap = (swap_f, x)
    sends = []

    def send(src, dst, idx, to):
        copy = pltpu.make_async_remote_copy(
            src_ref=src,
            dst_ref=dst,
            send_sem=send_sem.at[idx],
            recv_sem=recv_sem.at[idx],
            device_id=to,
            device_id_type=MESH,
        )
        copy.start()
        sends.append(copy)

    def recv(dst, idx):
        pltpu.make_async_remote_copy(
            src_ref=dst,
            dst_ref=dst,
            send_sem=send_sem.at[idx],
            recv_sem=recv_sem.at[idx],
            device_id=ypair,
            device_id_type=MESH,
        ).wait_recv()

    events = []

    def at(time, fn):
        events.append((time, len(events), fn))

    local = [
        pltpu.make_async_copy(wq_hbm, wbuf.at[x, yl, z, :, pl.ds(0, QW)], local_sem.at[0]),
        pltpu.make_async_copy(wk_hbm, wbuf.at[x, yl, z, :, pl.ds(QW, 128)], local_sem.at[1]),
        pltpu.make_async_copy(wv_hbm, wbuf.at[x, yl, z, :, pl.ds(QW + 128, 128)], local_sem.at[2]),
        pltpu.make_async_copy(tok_hbm, xall.at[t], local_sem.at[3]),
    ]
    for copy in local:
        copy.start()

    barrier = pltpu.get_barrier_semaphore()
    partners = [
        dev(dx=1), dev(dx=3), dev(dz=1), dev(dz=3), dev(dy=1), dev(dy=3),
        dev(flip=1), dev(dy=2), dev(dy=2, flip=1),
    ]
    for to in partners:
        pl.semaphore_signal(barrier, inc=1, device_id=to, device_id_type=MESH)

    @pl.when(x != t)
    def _():
        pl.semaphore_signal(barrier, inc=1, device_id=swap, device_id_type=MESH)

    pl.semaphore_wait(barrier, len(partners) + jnp.where(x != t, 1, 0))

    def gather(buf, base, times):
        def slot(color, da, yy, db):
            dx, dz = (da, db) if color == 0 else (db, da)
            rows = pl.ds(color * 80, 80)
            return buf.at[(x + dx) % 4, yy, (z + dz) % 4, rows]

        def pair(color, da, db):
            dx, dz = (da, db) if color == 0 else (db, da)
            rows = pl.ds(color * 80, 80)
            return buf.at[(x + dx) % 4, :, (z + dz) % 4, rows]

        def step(color, stage, sign):
            d = sign % 4
            along_x = (stage == 0) == (color == 0)
            return dev(dx=d) if along_x else dev(dz=d)

        def sem(color, k):
            return base + 1 + color * 22 + k

        def e0():
            own = buf.at[x, yl, z]
            send(own, own, base, ypair)
            for c in range(2):
                send(slot(c, 0, yl, 0), slot(c, 0, yl, 0), sem(c, 0), step(c, 0, 1))
                send(slot(c, 0, yl, 0), slot(c, 0, yl, 0), sem(c, 1), step(c, 0, -1))

        def second(c, da, k):
            send(pair(c, da, 0), pair(c, da, 0), sem(c, 6 + 4 * k), step(c, 1, 1))
            send(pair(c, da, 0), pair(c, da, 0), sem(c, 7 + 4 * k), step(c, 1, -1))

        def e1():
            recv(buf.at[x, 1 - yl, z], base)
            for c in range(2):
                send(slot(c, 0, 1 - yl, 0), slot(c, 0, 1 - yl, 0), sem(c, 2), step(c, 0, 1))
                send(slot(c, 0, 1 - yl, 0), slot(c, 0, 1 - yl, 0), sem(c, 3), step(c, 0, -1))
            for c in range(2):
                second(c, 0, 0)

        def e2():
            for c in range(2):
                recv(slot(c, 3, yl, 0), sem(c, 0))
                recv(slot(c, 1, yl, 0), sem(c, 1))
                recv(slot(c, 3, 1 - yl, 0), sem(c, 2))
                recv(slot(c, 1, 1 - yl, 0), sem(c, 3))
                send(slot(c, 3, 0, 0), slot(c, 3, 0, 0), sem(c, 4), step(c, 0, 1))
                send(slot(c, 1, 1, 0), slot(c, 1, 1, 0), sem(c, 5), step(c, 0, -1))
            for c in range(2):
                second(c, 3, 1)
            for c in range(2):
                second(c, 1, 2)

        def e3():
            for c in range(2):
                recv(slot(c, 2, 0, 0), sem(c, 4))
                recv(slot(c, 2, 1, 0), sem(c, 5))
                second(c, 2, 3)

        order = (0, 3, 1, 2)

        def e4(k):
            da = order[k]
            for c in range(2):
                recv(pair(c, da, 3), sem(c, 6 + 4 * k))
                recv(pair(c, da, 1), sem(c, 7 + 4 * k))
                send(slot(c, da, 0, 3), slot(c, da, 0, 3), sem(c, 8 + 4 * k), step(c, 1, 1))
                send(slot(c, da, 1, 1), slot(c, da, 1, 1), sem(c, 9 + 4 * k), step(c, 1, -1))

        def e5(k):
            da = order[k]
            for c in range(2):
                recv(slot(c, da, 0, 2), sem(c, 8 + 4 * k))
                recv(slot(c, da, 1, 2), sem(c, 9 + 4 * k))

        fns = (
            e0, e1, e2, e3,
            lambda: e4(0), lambda: e4(1), lambda: e4(2), lambda: e4(3),
            lambda: e5(0), lambda: e5(1), lambda: e5(2), lambda: e5(3),
        )
        for when, fn in zip(times, fns):
            at(when, fn)

    def origin_hi(dy):
        return ((y + dy) % 4) // 2

    def rows_out(buf, stage, base, n, chunk, i, src=None):
        rows = pl.ds(i * chunk, chunk)
        srows = pl.ds((i // 2) * chunk, chunk)
        own = buf.at[t, rows] if src is None else src.at[rows]
        d = 1 if i % 2 == 0 else 3
        send(own, stage.at[i % 2, srows], base + 4 * i, dev(dy=d))
        send(own, buf.at[t, rows], base + 4 * i + 1, dev(flip=1))

    def rows_relay(buf, stage, base, n, chunk, i):
        rows = pl.ds(i * chunk, chunk)
        srows = pl.ds((i // 2) * chunk, chunk)
        d = 1 if i % 2 == 0 else 3
        recv(stage.at[i % 2, srows], base + 4 * i)
        came = origin_hi(4 - d) * 2 + core
        send(stage.at[i % 2, srows], buf.at[came, rows], base + 4 * i + 2, dev(dy=d))

    def rows_in(buf, stage, base, n, chunk, i):
        rows = pl.ds(i * chunk, chunk)
        far = (t + 2) % 4
        recv(buf.at[far, rows], base + 4 * i + 2)
        send(buf.at[far, rows], buf.at[far, rows], base + 4 * i + 3, dev(flip=1))

    def rows_done(buf, stage, base, n, chunk, i):
        rows = pl.ds(i * chunk, chunk)
        sib = (core + 1) % 2
        recv(buf.at[yh * 2 + sib, rows], base + 4 * i + 1)
        recv(buf.at[(1 - yh) * 2 + sib, rows], base + 4 * i + 3)

    tok = (xall, xstage, SEM_T, TOK_N, TOK_CHUNK)
    atd = (att, astage, SEM_A, ATT_N, ATT_CHUNK)

    def exchange(k):
        for n, to in enumerate((dev(flip=1), dev(dy=2), dev(dy=2, flip=1))):
            send(sqt.at[k, pl.ds(0, 8)], sqr.at[k, n], SEM_S + 3 * k + n, to)

    def exchanged(k):
        total = sqt[k, pl.ds(0, 8)]
        for n in range(3):
            recv(sqr.at[k, n], SEM_S + 3 * k + n)
            total = total + sqr[k, n]
        return jnp.concatenate([total] * 16, axis=0).T

    def qkv(p, dx, first):
        j = (x + dx) % 4
        rows = pl.ds(p * HALF, HALF)
        part = jnp.dot(
            xall[j, rows], wbuf[j].reshape(TCOL, QKV), preferred_element_type=jnp.float32
        )
        if first:
            acc[rows] = part
        else:
            acc[rows] += part

    lane = lax.broadcasted_iota(jnp.int32, (HALF, 128), 1)

    def sums(p):
        rows = pl.ds(p * HALF, HALF)
        q = acc[rows, pl.ds(0, QW)]
        k = acc[rows, pl.ds(QW, 128)]
        qs = jnp.sum(q * q, axis=1, keepdims=True)
        ks = jnp.sum(k * k, axis=1, keepdims=True)
        both = jnp.where(lane < 4, qs, ks)
        sqt[0, :, rows] = both.T

    def rotate():
        total = exchanged(0)
        res_q = lax.rsqrt(total[:, 0:1] / (HEADS * HEAD_DIM) + EPS)
        res_k = lax.rsqrt(total[:, 4:5] / (KV_HEADS * HEAD_DIM) + EPS)
        for h in range(6):
            cols = pl.ds(h * 128, 128)
            u = acc[:, cols] * (res_q if h < 5 else res_k) * gain_ref[:, cols]
            r = u * cos_ref[...] + pltpu.roll(u, 64, 1) * sin_ref[...]
            rot[:, cols] = r.astype(jnp.bfloat16)
        vbuf[...] = acc[:, pl.ds(QW + 128, 128)].astype(jnp.bfloat16)

    def attend(p, b):
        rows = pl.ds(p * HALF + b * 128, 128)
        width = (b + 1) * 128
        seen = pl.ds(p * HALF, width)
        kk = rot[seen, pl.ds(QW, 128)]
        vv = vbuf[seen]
        first = start_ref[rows] - p * HALF
        col = lax.broadcasted_iota(jnp.int32, (128, width), 1)
        row = lax.broadcasted_iota(jnp.int32, (128, width), 0) + b * 128
        allowed = (col >= first) & (col <= row)
        for h in range(5):
            cols = pl.ds(h * 128, 128)
            s = lax.dot_general(
                rot[rows, cols], kk, (((1,), (1,)), ((), ())), preferred_element_type=jnp.float32
            )
            s = jnp.where(allowed, s * (1.0 / math.sqrt(HEAD_DIM)), jnp.float32(-1e30))
            e = jnp.exp(s - jnp.max(s, axis=1, keepdims=True))
            probs = (e * (1.0 / jnp.sum(e, axis=1, keepdims=True))).astype(jnp.bfloat16)
            o = jnp.dot(probs, vv, preferred_element_type=jnp.float32)
            att[t, rows, cols] = o.astype(jnp.bfloat16)

    def project(p, j, first):
        rows = pl.ds(p * HALF, HALF)
        part = lax.dot_general(
            att[j, rows],
            obuf[j].reshape(TCOL, QW),
            (((1,), (1,)), ((), ())),
            preferred_element_type=jnp.float32,
        )
        if first:
            oacc[rows] = part
        else:
            oacc[rows] += part

    def out_sums(p):
        rows = pl.ds(p * HALF, HALF)
        o = oacc[rows]
        sqt[1, :, rows] = jnp.broadcast_to(jnp.sum(o * o, axis=1, keepdims=True), (HALF, 128)).T

    def finish():
        total = exchanged(1)
        live = live_ref[0]
        for p in range(2):
            rows = pl.ds(p * HALF, HALF)
            scale = lax.rsqrt(total[p * HALF : (p + 1) * HALF, 0:1] / D + EPS)
            r = xall[t, rows].astype(jnp.float32) + oacc[rows] * scale * ogain_ref[...]
            row = lax.broadcasted_iota(jnp.int32, (HALF, TCOL), 0) + p * HALF
            res[rows] = jnp.where(row < live, r, 0.0).astype(jnp.bfloat16)
        done = pltpu.make_async_copy(res, out_hbm, local_sem.at[0])
        done.start()
        done.wait()

    for copy in local[:3]:
        copy.wait()
    gather(wbuf, SEM_W, (0, 8, 12, 20, 19, 26, 32, 38, 32.5, 40, 44, 50))

    own_o = obuf.at[x, yl, z]

    def swap_out():
        @pl.when(x != t)
        def _():
            copy = pltpu.make_async_remote_copy(
                src_ref=wot_hbm, dst_ref=obuf.at[t, yl, z], send_sem=send_sem.at[SEM_P],
                recv_sem=recv_sem.at[SEM_P], device_id=swap, device_id_type=MESH,
            )
            copy.start()

        @pl.when(x == t)
        def _():
            copy = pltpu.make_async_copy(wot_hbm, own_o, local_sem.at[4])
            copy.start()

    def swap_in():
        @pl.when(x != t)
        def _():
            copy = pltpu.make_async_remote_copy(
                src_ref=wot_hbm, dst_ref=own_o, send_sem=send_sem.at[SEM_P],
                recv_sem=recv_sem.at[SEM_P], device_id=swap, device_id_type=MESH,
            )
            copy.wait()

        @pl.when(x == t)
        def _():
            copy = pltpu.make_async_copy(wot_hbm, own_o, local_sem.at[4])
            copy.wait()

    at(1.5, swap_out)
    for i in range(TOK_N):
        at(1.0, functools.partial(rows_out, *tok, i, tok_hbm))
        at(10 + 7 * (i // 2), functools.partial(rows_relay, *tok, i))
        at(17 + 7 * (i // 2), functools.partial(rows_in, *tok, i))
    for i in range(TOK_N // 2):
        at(33, functools.partial(rows_done, *tok, i))
    at(33.1, lambda: local[3].wait())
    at(33.2, functools.partial(qkv, 0, 0, True))
    for i in range(TOK_N // 2, TOK_N):
        at(53, functools.partial(rows_done, *tok, i))
    at(53.1, functools.partial(qkv, 1, 0, True))
    for n, dx in enumerate((3, 1, 2)):
        for p in range(2):
            at(53.2 + n / 10, functools.partial(qkv, p, dx, False))

    at(39, swap_in)
    gather(obuf, SEM_O, (39.1, 46, 53.15, 58, 58, 61, 62.5, 64, 69, 70, 72, 82))

    at(54, lambda: sums(0))
    at(54, lambda: sums(1))
    at(54.1, lambda: exchange(0))
    at(60, rotate)
    for i in range(ATT_N):
        at(63 + 2.5 * i, functools.partial(attend, i // 3, i % 3))
        at(63.1 + 2.5 * i, functools.partial(rows_out, *atd, i))
        at(69 + 2.5 * i, functools.partial(rows_relay, *atd, i))
        at(75 + 2.5 * i, functools.partial(rows_in, *atd, i))
    for p in range(2):
        at(82.5, functools.partial(project, p, t, True))
    for i in range(ATT_N):
        at(88, functools.partial(rows_done, *atd, i))
    for n in range(1, 4):
        for p in range(2):
            at(89 + n / 10, functools.partial(project, p, (t + n) % 4, False))
    at(95, lambda: out_sums(0))
    at(95, lambda: out_sums(1))
    at(95.1, lambda: exchange(1))
    at(96, finish)

    for _, _, fn in sorted(events, key=lambda e: (e[0], e[1])):
        fn()
    for copy in sends:
        copy.wait_send()


def body(
    tokens, live_rows, first_row, w_query, w_key, w_value, w_out, query_gain, key_gain, out_gain
):
    half = HEAD_DIM // 2
    freqs = jnp.power(ROPE_BASE, -(jnp.arange(half, dtype=jnp.float32) * 2.0 / HEAD_DIM))
    positions = (jnp.arange(CAP, dtype=jnp.int32) - first_row).astype(jnp.float32)
    angle = positions[:, None] * freqs[None, :]
    cosine, sine = jnp.cos(angle), jnp.sin(angle)
    cos = jnp.concatenate([cosine, cosine], axis=1)
    sin = jnp.concatenate([-sine, sine], axis=1)
    gains = jnp.concatenate([query_gain, key_gain])[None, :]
    hbm = pl.BlockSpec(memory_space=pl.ANY)
    vmem = pl.BlockSpec(memory_space=pltpu.VMEM)
    smem = pl.BlockSpec(memory_space=pltpu.SMEM)
    bf, fl = jnp.bfloat16, jnp.float32
    return pl.pallas_call(
        kernel,
        out_shape=jax.ShapeDtypeStruct((CAP, TCOL), bf),
        in_specs=[hbm] * 5 + [vmem] * 5 + [smem],
        out_specs=hbm,
        scratch_shapes=[
            pltpu.VMEM((4, 2, 4, SHARD, QKV), bf),
            pltpu.VMEM((4, 2, 4, SHARD, QW), bf),
            pltpu.VMEM((4, CAP, TCOL), bf),
            pltpu.VMEM((2, HALF, TCOL), bf),
            pltpu.VMEM((CAP, QKV), fl),
            pltpu.VMEM((CAP, QW + 128), bf),
            pltpu.VMEM((CAP, 128), bf),
            pltpu.VMEM((4, CAP, QW), bf),
            pltpu.VMEM((2, HALF, QW), bf),
            pltpu.VMEM((CAP, TCOL), fl),
            pltpu.VMEM((CAP, TCOL), bf),
            pltpu.VMEM((2, 128, CAP), fl),
            pltpu.VMEM((2, 3, 8, CAP), fl),
            pltpu.SemaphoreType.DMA((SEM_N,)),
            pltpu.SemaphoreType.DMA((SEM_N,)),
            pltpu.SemaphoreType.DMA((5,)),
        ],
        compiler_params=pltpu.CompilerParams(
            collective_id=0, has_side_effects=True, vmem_limit_bytes=60 * 1024 * 1024
        ),
    )(
        tokens,
        w_query,
        w_key,
        w_value,
        w_out.T,
        cos,
        sin,
        first_row[:, None],
        gains,
        out_gain[None, :],
        live_rows,
    )


def solution(mesh):
    in_specs = (
        P("fsdp", "tensor"),
        P("fsdp"),
        P("fsdp"),
        P("fsdp", "tensor"),
        P("fsdp", "tensor"),
        P("fsdp", "tensor"),
        P("tensor", "fsdp"),
        P("tensor"),
        P("tensor"),
        P("tensor"),
    )
    return jax.shard_map(
        body, mesh=mesh, in_specs=in_specs, out_specs=P("fsdp", "tensor"), check_vma=False
    )
```

```python
import functools
import math

import jax
import jax.numpy as jnp
from jax import lax
from jax.experimental import pallas as pl
from jax.experimental.pallas import tpu as pltpu
from jax.sharding import PartitionSpec as P

D = 5120
HEADS = 20
KV_HEADS = 4
HEAD_DIM = 128
CAP = 768
HALF = 384
EPS = 1e-06
ROPE_BASE = 500000.0
SHARD = 160
QKV = 896
QW = 640
TCOL = 1280
MESH = pl.DeviceIdType.MESH

TOK_CHUNK = 64
TOK_N = CAP // TOK_CHUNK
ATT_CHUNK = 128
ATT_N = CAP // ATT_CHUNK

AG_SEMS = 2 * 24 + 2
SEM_W = 0
SEM_O = SEM_W + AG_SEMS
SEM_T = SEM_O + AG_SEMS
SEM_A = SEM_T + 4 * TOK_N
SEM_S = SEM_A + 4 * ATT_N
SEM_P = SEM_S + 6
SEM_N = SEM_P + 1


def plan(events, rate=45.0, hop=1.8, report=None):
    now, done, arrive, free, order = 0.0, set(), {}, {}, []
    left = list(events)
    while left:
        best = None
        for n, (name, after, waits, sends, cost, late, work) in enumerate(left):
            if any(a not in done for a in after) or any(i not in arrive for i, _ in waits):
                continue
            ready = max([now] + [arrive[i] for i, _ in waits])
            key = (ready, late, n)
            if best is None or key < best[0]:
                best = (key, n)
        (ready, _, _), n = best
        name, after, waits, sends, cost, late, work = left.pop(n)
        now = ready + cost + 0.02
        for idx, link, kb, _ in sends:
            lines = ("y+", "y-") if link == "yp" else (link,)
            begin = max([now] + [free.get(line, 0.0) for line in lines])
            speed = 200.0 if link == "c" else rate
            finish = begin + kb / speed
            for line in lines:
                free[line] = finish if len(lines) == 1 else max(free.get(line, 0.0), finish)
            arrive[idx] = finish + (1.0 if link == "c" else 2 * hop if link == "far" else hop)
        done.add(name)
        order.append(name)
        if report is not None:
            report.append((name, now))
    return order


def kernel(
    tok_hbm,
    wq_hbm,
    wk_hbm,
    wv_hbm,
    wot_hbm,
    cos_ref,
    sin_ref,
    start_ref,
    gain_ref,
    ogain_ref,
    live_ref,
    out_hbm,
    wbuf,
    obuf,
    xall,
    xstage,
    acc,
    rot,
    vbuf,
    att,
    astage,
    oacc,
    res,
    sqt,
    sqr,
    krow,
    qcol,
    send_sem,
    recv_sem,
    local_sem,
):
    f = lax.axis_index("fsdp")
    t = lax.axis_index("tensor")
    x, yl, z = f // 8, (f // 4) % 2, f % 4
    yh, core = t // 2, t % 2
    y = 2 * yh + yl

    def dev(dx=0, dy=0, dz=0, flip=0):
        ny = (y + dy) % 4
        nf = ((x + dx) % 4) * 8 + (ny % 2) * 4 + (z + dz) % 4
        nc = (core + flip) % 2
        return (nf, (ny // 2) * 2 + nc)

    ypair = ((x * 8 + (1 - yl) * 4 + z), t)
    swap_f = t * 8 + yl * 4 + z
    swap = (swap_f, x)
    sends = []

    def send(src, dst, idx, to):
        copy = pltpu.make_async_remote_copy(
            src_ref=src,
            dst_ref=dst,
            send_sem=send_sem.at[idx],
            recv_sem=recv_sem.at[idx],
            device_id=to,
            device_id_type=MESH,
        )
        copy.start()
        sends.append(copy)

    def recv(dst, idx):
        pltpu.make_async_remote_copy(
            src_ref=dst,
            dst_ref=dst,
            send_sem=send_sem.at[idx],
            recv_sem=recv_sem.at[idx],
            device_id=ypair,
            device_id_type=MESH,
        ).wait_recv()

    events = []

    def event(name, after=(), waits=(), sends=(), cost=0.0, late=0, work=None):
        events.append((name, tuple(after), tuple(waits), tuple(sends), cost, late, work))

    def run():
        for name in plan(events):
            _, _, waits, outs, _, _, work = next(e for e in events if e[0] == name)
            for idx, dst in waits:
                recv(dst(), idx)
            if work is not None:
                work()
            for idx, _, _, what in outs:
                what(idx)

    local = [
        pltpu.make_async_copy(wq_hbm, wbuf.at[x, yl, z, :, pl.ds(0, QW)], local_sem.at[0]),
        pltpu.make_async_copy(wk_hbm, wbuf.at[x, yl, z, :, pl.ds(QW, 128)], local_sem.at[1]),
        pltpu.make_async_copy(wv_hbm, wbuf.at[x, yl, z, :, pl.ds(QW + 128, 128)], local_sem.at[2]),
        pltpu.make_async_copy(tok_hbm, xall.at[t], local_sem.at[3]),
    ]
    for copy in local:
        copy.start()

    barrier = pltpu.get_barrier_semaphore()
    partners = [
        dev(dx=1), dev(dx=3), dev(dz=1), dev(dz=3), dev(dy=1), dev(dy=3),
        dev(flip=1), dev(dy=2), dev(dy=2, flip=1),
    ]
    for to in partners:
        pl.semaphore_signal(barrier, inc=1, device_id=to, device_id_type=MESH)

    @pl.when(x != t)
    def _():
        pl.semaphore_signal(barrier, inc=1, device_id=swap, device_id_type=MESH)

    pl.semaphore_wait(barrier, len(partners) + jnp.where(x != t, 1, 0))

    def gather(tag, buf, base, kb, start, start_y):
        order = (0, 3, 1, 2)

        def slot(color, da, yy, db):
            dx, dz = (da, db) if color == 0 else (db, da)
            return buf.at[(x + dx) % 4, yy, (z + dz) % 4, pl.ds(color * 80, 80)]

        def pair(color, da, db):
            dx, dz = (da, db) if color == 0 else (db, da)
            return buf.at[(x + dx) % 4, :, (z + dz) % 4, pl.ds(color * 80, 80)]

        def out(color, stage, sign, k, ref, units=1):
            along_x = (stage == 0) == (color == 0)
            d = sign % 4
            to = dev(dx=d) if along_x else dev(dz=d)
            link = ("x" if along_x else "z") + ("+" if sign > 0 else "-")
            return (base + 24 * color + k, link, units * kb, lambda idx: send(ref(), ref(), idx, to))

        def second(c, k):
            da = order[k]
            return [
                out(c, 1, 1, 6 + 4 * k, lambda: pair(c, da, 0), 2),
                out(c, 1, -1, 7 + 4 * k, lambda: pair(c, da, 0), 2),
            ]

        def half(c, yy):
            return buf.at[x, yy, z, pl.ds(c * 80, 80)]

        for c in range(2):
            event(
                f"{tag}y{c}", start_y,
                sends=[(base + 48 + c, "yp", kb, lambda idx, c=c: send(half(c, yl), half(c, yl), idx, ypair))],
            )
        for stage in range(2):
            for c in range(2):
                k = 0 if stage == 0 else 6
                own = functools.partial(half, c, yl)
                event(
                    f"{tag}0{stage}{c}", start,
                    sends=[out(c, stage, 1, k, own), out(c, stage, -1, k + 1, own)],
                )
        for c in range(2):
            sem = base + 24 * c
            other = functools.partial(half, c, 1 - yl)
            event(
                f"{tag}1{c}", start,
                waits=[(base + 48 + c, other)],
                sends=[
                    out(c, 0, 1, 2, other), out(c, 0, -1, 3, other),
                    out(c, 1, 1, 22, other), out(c, 1, -1, 23, other),
                ],
            )
            event(
                f"{tag}2l{c}",
                waits=[(sem, lambda c=c: slot(c, 3, yl, 0)), (sem + 2, lambda c=c: slot(c, 3, 1 - yl, 0))],
                sends=[out(c, 0, 1, 4, lambda c=c: slot(c, 3, 0, 0))] + second(c, 1),
            )
            event(
                f"{tag}2r{c}",
                waits=[(sem + 1, lambda c=c: slot(c, 1, yl, 0)), (sem + 3, lambda c=c: slot(c, 1, 1 - yl, 0))],
                sends=[out(c, 0, -1, 5, lambda c=c: slot(c, 1, 1, 0))] + second(c, 2),
            )
            event(
                f"{tag}3{c}",
                waits=[(sem + 4, lambda c=c: slot(c, 2, 0, 0)), (sem + 5, lambda c=c: slot(c, 2, 1, 0))],
                sends=second(c, 3),
            )
            for k in range(4):
                da = order[k]
                left = [(sem + 6 + 4 * k, lambda c=c, da=da: pair(c, da, 3))]
                right = [(sem + 7 + 4 * k, lambda c=c, da=da: pair(c, da, 1))]
                if k == 0:
                    left = [
                        (sem + 6, lambda c=c: slot(c, 0, yl, 3)), (sem + 22, lambda c=c: slot(c, 0, 1 - yl, 3)),
                    ]
                    right = [
                        (sem + 7, lambda c=c: slot(c, 0, yl, 1)), (sem + 23, lambda c=c: slot(c, 0, 1 - yl, 1)),
                    ]
                event(
                    f"{tag}4l{c}{k}", waits=left,
                    sends=[out(c, 1, 1, 8 + 4 * k, lambda c=c, da=da: slot(c, da, 0, 3))],
                )
                event(
                    f"{tag}4r{c}{k}", waits=right,
                    sends=[out(c, 1, -1, 9 + 4 * k, lambda c=c, da=da: slot(c, da, 1, 1))],
                )
                event(
                    f"{tag}5{c}{k}",
                    waits=[
                        (sem + 8 + 4 * k, lambda c=c, da=da: slot(c, da, 0, 2)),
                        (sem + 9 + 4 * k, lambda c=c, da=da: slot(c, da, 1, 2)),
                    ],
                )

    def plane(tag, dx):
        k = (0, 3, 1, 2).index(dx)
        need = [f"{tag}4l0{k}", f"{tag}4r0{k}", f"{tag}50{k}", f"{tag}2l0", f"{tag}2r0", f"{tag}30"]
        if dx == 0:
            need += [f"{tag}11", f"{tag}2l1", f"{tag}2r1", f"{tag}31"]
        else:
            need += [f"{tag}" + {3: "4l1", 1: "4r1", 2: "51"}[dx] + f"{n}" for n in range(4)]
        return need + [f"{tag}10", f"{tag}11"]

    def spread(tag, buf, stage, base, chunk, i, kb, after, src=None):
        rows = pl.ds(i * chunk, chunk)
        held = stage.at[i % 2, pl.ds((i // 2) * chunk, chunk)]
        own = buf.at[t, rows] if src is None else src.at[rows]
        d, back, link = (1, 3, "y+") if i % 2 == 0 else (3, 1, "y-")
        came = (((y + back) % 4) // 2) * 2 + core
        far = (t + 2) % 4
        sib = (core + 1) % 2
        base = base + 4 * i
        event(
            f"{tag}o{i}", after,
            sends=[
                (base, link, kb, lambda idx: send(own, held, idx, dev(dy=d))),
                (base + 1, "c", kb, lambda idx: send(own, buf.at[t, rows], idx, dev(flip=1))),
            ],
        )
        event(
            f"{tag}r{i}", waits=[(base, lambda: held)],
            sends=[(base + 2, link, kb, lambda idx: send(held, buf.at[came, rows], idx, dev(dy=d)))],
        )
        event(
            f"{tag}i{i}", waits=[(base + 2, lambda: buf.at[far, rows])],
            sends=[(base + 3, "c", kb, lambda idx: send(buf.at[far, rows], buf.at[far, rows], idx, dev(flip=1)))],
        )
        event(
            f"{tag}d{i}",
            waits=[
                (base + 1, lambda: buf.at[yh * 2 + sib, rows]),
                (base + 3, lambda: buf.at[(1 - yh) * 2 + sib, rows]),
            ],
        )

    def exchange(k, after):
        outs = []
        for n, to in enumerate((dev(flip=1), dev(dy=2), dev(dy=2, flip=1))):
            outs.append((
                SEM_S + 3 * k + n, "c" if n == 0 else "far", 12,
                lambda idx, n=n, to=to: send(sqt.at[k, pl.ds(0, 8)], sqr.at[k, n], idx, to),
            ))
        event(f"x{k}", after, sends=outs)

    def exchanged(k):
        return [(SEM_S + 3 * k + n, lambda n=n: sqr.at[k, n]) for n in range(3)]

    def total(k):
        return sqt[k, pl.ds(0, 8)] + sqr[k, 0] + sqr[k, 1] + sqr[k, 2]

    def qkv(p, dx, first):
        j = (x + dx) % 4
        rows = pl.ds(p * HALF, HALF)
        part = jnp.dot(
            xall[j, rows], wbuf[j].reshape(TCOL, QKV), preferred_element_type=jnp.float32
        )
        if first:
            acc[rows] = part
        else:
            acc[rows] += part

    lane = lax.broadcasted_iota(jnp.int32, (HALF, 128), 1)

    def sums(p):
        rows = pl.ds(p * HALF, HALF)
        q = acc[rows, pl.ds(0, QW)]
        k = acc[rows, pl.ds(QW, 128)]
        qs = jnp.sum(q * q, axis=1, keepdims=True)
        ks = jnp.sum(k * k, axis=1, keepdims=True)
        both = jnp.where(lane < 4, qs, ks)
        sqt[0, :, rows] = both.T

    def rotate(p):
        rows = pl.ds(p * HALF, HALF)
        for h in range(6):
            cols = pl.ds(h * 128, 128)
            u = acc[rows, cols] * gain_ref[:, cols]
            r = u * cos_ref[rows] + pltpu.roll(u, 64, 1) * sin_ref[rows]
            rot[rows, cols] = r.astype(jnp.bfloat16)
        vbuf[rows] = acc[rows, pl.ds(QW + 128, 128)].astype(jnp.bfloat16)

    def scales():
        sq = total(0)
        res_q = lax.rsqrt(sq[0:4] / (HEADS * HEAD_DIM) + EPS) * (1.0 / math.sqrt(HEAD_DIM))
        res_k = lax.rsqrt(sq[4:8] / (KV_HEADS * HEAD_DIM) + EPS)
        both = jnp.concatenate([res_q, res_k], axis=0)
        krow[...] = both
        qcol[...] = jnp.concatenate([both] * 16, axis=0).T

    def attend(p, b):
        rows = pl.ds(p * HALF + b * 128, 128)
        width = (b + 1) * 128
        seen = pl.ds(p * HALF, width)
        kk = rot[seen, pl.ds(QW, 128)]
        vv = vbuf[seen]
        first = start_ref[rows] - p * HALF
        col = lax.broadcasted_iota(jnp.int32, (128, width), 1)
        row = lax.broadcasted_iota(jnp.int32, (128, width), 0) + b * 128
        allowed = (col >= first) & (col <= row)
        scale = qcol[rows, 0:1] * krow[4:5, p * HALF : p * HALF + width]
        for h in range(5):
            cols = pl.ds(h * 128, 128)
            s = lax.dot_general(
                rot[rows, cols], kk, (((1,), (1,)), ((), ())), preferred_element_type=jnp.float32
            )
            s = jnp.where(allowed, s * scale, jnp.float32(-1e30))
            e = jnp.exp(s - jnp.max(s, axis=1, keepdims=True))
            probs = (e * (1.0 / jnp.sum(e, axis=1, keepdims=True))).astype(jnp.bfloat16)
            o = jnp.dot(probs, vv, preferred_element_type=jnp.float32)
            att[t, rows, cols] = o.astype(jnp.bfloat16)

    def project(p, dx, first):
        j = (x + dx) % 4
        rows = pl.ds(p * HALF, HALF)
        part = lax.dot_general(
            att[j, rows],
            obuf[j].reshape(TCOL, QW),
            (((1,), (1,)), ((), ())),
            preferred_element_type=jnp.float32,
        )
        if first:
            oacc[rows] = part
        else:
            oacc[rows] += part

    def out_sums(p):
        rows = pl.ds(p * HALF, HALF)
        o = oacc[rows]
        sqt[1, :, rows] = jnp.broadcast_to(jnp.sum(o * o, axis=1, keepdims=True), (HALF, 128)).T

    def finish():
        sums_out = jnp.concatenate([total(1)] * 16, axis=0).T
        live = live_ref[0]
        for p in range(2):
            rows = pl.ds(p * HALF, HALF)
            scale = lax.rsqrt(sums_out[p * HALF : (p + 1) * HALF, 0:1] / D + EPS)
            r = xall[t, rows].astype(jnp.float32) + oacc[rows] * scale * ogain_ref[...]
            row = lax.broadcasted_iota(jnp.int32, (HALF, TCOL), 0) + p * HALF
            res[rows] = jnp.where(row < live, r, 0.0).astype(jnp.bfloat16)
        done = pltpu.make_async_copy(res, out_hbm, local_sem.at[0])
        done.start()
        done.wait()

    for copy in local[:3]:
        copy.wait()

    own_o = obuf.at[x, yl, z]

    def swap_out():
        @pl.when(x != t)
        def _():
            copy = pltpu.make_async_remote_copy(
                src_ref=wot_hbm, dst_ref=obuf.at[t, yl, z], send_sem=send_sem.at[SEM_P],
                recv_sem=recv_sem.at[SEM_P], device_id=swap, device_id_type=MESH,
            )
            copy.start()

        @pl.when(x == t)
        def _():
            copy = pltpu.make_async_copy(wot_hbm, own_o, local_sem.at[4])
            copy.start()

    def swap_in():
        @pl.when(x != t)
        def _():
            copy = pltpu.make_async_remote_copy(
                src_ref=wot_hbm, dst_ref=own_o, send_sem=send_sem.at[SEM_P],
                recv_sem=recv_sem.at[SEM_P], device_id=swap, device_id_type=MESH,
            )
            copy.wait()

        @pl.when(x == t)
        def _():
            copy = pltpu.make_async_copy(wot_hbm, own_o, local_sem.at[4])
            copy.wait()

    w_sends = [f"w4{s}{c}{k}" for s in "lr" for c in range(2) for k in range(4)]
    gather("w", wbuf, SEM_W, 143.4, (), ())
    event("swap", ("w010", "w011"), sends=[(SEM_P, "far", 205, lambda idx: swap_out())])
    for i in range(TOK_N):
        spread("t", xall, xstage, SEM_T, TOK_CHUNK, i, 163.8, ("wy0", "wy1", "w010", "w011"), tok_hbm)
    event("swapped", ("swap", "tr5"), cost=0.1, work=swap_in)
    gather("o", obuf, SEM_O, 102.4, ["swapped"] + w_sends, ["swapped"])
    event("own", work=local[3].wait)

    half_t = TOK_N // 2
    last = {}
    for p in range(2):
        rows_in = ["own"] + [f"t{s}{p * half_t + i}" for s in "rid" for i in range(half_t)]
        for n, dx in enumerate((0, 3, 1, 2)):
            event(
                f"q{p}{n}", rows_in + plane("w", dx) + ([f"q{p}{n - 1}"] if n else []),
                cost=1.2, late=1, work=functools.partial(qkv, p, dx, n == 0),
            )
        event(f"sum{p}", [f"q{p}3"], cost=0.4, late=1, work=functools.partial(sums, p))
    exchange(0, ("sum0", "sum1"))
    for p in range(2):
        event(f"rot{p}", ("x0",), cost=1.0, late=1, work=functools.partial(rotate, p))
    event("scale", ("rot0", "rot1"), waits=exchanged(0), cost=0.4, late=1, work=scales)
    prev = "scale"
    half_a = ATT_N // 2
    for i in range(ATT_N):
        event(f"att{i}", (prev,), cost=0.8, late=1, work=functools.partial(attend, i // 3, i % 3))
        spread("a", att, astage, SEM_A, ATT_CHUNK, i, 163.8, (f"att{i}",))
        prev = f"att{i}"
    for p in range(2):
        rows_in = [f"a{s}{p * half_a + i}" for s in "orid" for i in range(half_a)]
        for n, dx in enumerate((0, 3, 1, 2)):
            event(
                f"p{p}{n}", rows_in + plane("o", dx) + ([f"p{p}{n - 1}"] if n else []),
                cost=0.9, late=1, work=functools.partial(project, p, dx, n == 0),
            )
        event(f"osum{p}", [f"p{p}3"], cost=0.3, late=1, work=functools.partial(out_sums, p))
    exchange(1, ("osum0", "osum1"))
    event("end", ("x1",), waits=exchanged(1), cost=3.0, late=1, work=finish)
    run()
    for copy in sends:
        copy.wait_send()


def body(
    tokens, live_rows, first_row, w_query, w_key, w_value, w_out, query_gain, key_gain, out_gain
):
    half = HEAD_DIM // 2
    freqs = jnp.power(ROPE_BASE, -(jnp.arange(half, dtype=jnp.float32) * 2.0 / HEAD_DIM))
    positions = (jnp.arange(CAP, dtype=jnp.int32) - first_row).astype(jnp.float32)
    angle = positions[:, None] * freqs[None, :]
    cosine, sine = jnp.cos(angle), jnp.sin(angle)
    cos = jnp.concatenate([cosine, cosine], axis=1)
    sin = jnp.concatenate([-sine, sine], axis=1)
    gains = jnp.concatenate([query_gain, key_gain])[None, :]
    hbm = pl.BlockSpec(memory_space=pl.ANY)
    vmem = pl.BlockSpec(memory_space=pltpu.VMEM)
    smem = pl.BlockSpec(memory_space=pltpu.SMEM)
    bf, fl = jnp.bfloat16, jnp.float32
    return pl.pallas_call(
        kernel,
        out_shape=jax.ShapeDtypeStruct((CAP, TCOL), bf),
        in_specs=[hbm] * 5 + [vmem] * 5 + [smem],
        out_specs=hbm,
        scratch_shapes=[
            pltpu.VMEM((4, 2, 4, SHARD, QKV), bf),
            pltpu.VMEM((4, 2, 4, SHARD, QW), bf),
            pltpu.VMEM((4, CAP, TCOL), bf),
            pltpu.VMEM((2, HALF, TCOL), bf),
            pltpu.VMEM((CAP, QKV), fl),
            pltpu.VMEM((CAP, QW + 128), bf),
            pltpu.VMEM((CAP, 128), bf),
            pltpu.VMEM((4, CAP, QW), bf),
            pltpu.VMEM((2, HALF, QW), bf),
            pltpu.VMEM((CAP, TCOL), fl),
            pltpu.VMEM((CAP, TCOL), bf),
            pltpu.VMEM((2, 128, CAP), fl),
            pltpu.VMEM((2, 3, 8, CAP), fl),
            pltpu.VMEM((8, CAP), fl),
            pltpu.VMEM((CAP, 128), fl),
            pltpu.SemaphoreType.DMA((SEM_N,)),
            pltpu.SemaphoreType.DMA((SEM_N,)),
            pltpu.SemaphoreType.DMA((5,)),
        ],
        compiler_params=pltpu.CompilerParams(
            collective_id=0, has_side_effects=True, vmem_limit_bytes=60 * 1024 * 1024
        ),
    )(
        tokens,
        w_query,
        w_key,
        w_value,
        w_out.T,
        cos,
        sin,
        first_row[:, None],
        gains,
        out_gain[None, :],
        live_rows,
    )


def solution(mesh):
    in_specs = (
        P("fsdp", "tensor"),
        P("fsdp"),
        P("fsdp"),
        P("fsdp", "tensor"),
        P("fsdp", "tensor"),
        P("fsdp", "tensor"),
        P("tensor", "fsdp"),
        P("tensor"),
        P("tensor"),
        P("tensor"),
    )
    return jax.shard_map(
        body, mesh=mesh, in_specs=in_specs, out_specs=P("fsdp", "tensor"), check_vma=False
    )
```

```python
import functools
import math

import jax
import jax.numpy as jnp
from jax import lax
from jax.experimental import pallas as pl
from jax.experimental.pallas import tpu as pltpu
from jax.sharding import PartitionSpec as P

D = 5120
HEADS = 20
KV_HEADS = 4
HEAD_DIM = 128
CAP = 768
HALF = 384
EPS = 1e-06
ROPE_BASE = 500000.0
SHARD = 160
QKV = 896
QW = 640
TCOL = 1280
MESH = pl.DeviceIdType.MESH

TOK_CHUNK = 64
TOK_N = CAP // TOK_CHUNK
ATT_CHUNK = 128
ATT_N = CAP // ATT_CHUNK

AG_SEMS = 2 * 24 + 2
SEM_W = 0
SEM_O = SEM_W + AG_SEMS
SEM_T = SEM_O + AG_SEMS
SEM_A = SEM_T + 4 * TOK_N
SEM_S = SEM_A + 4 * ATT_N
SEM_P = SEM_S + 12
SEM_N = SEM_P + 1


def plan(events, rate=45.0, hop=1.8, report=None):
    now, done, arrive, free, order = 0.0, set(), {}, {}, []
    left = list(events)
    while left:
        best = None
        for n, (name, after, waits, sends, cost, late, work) in enumerate(left):
            if any(a not in done for a in after) or any(i not in arrive for i, _ in waits):
                continue
            ready = max([now] + [arrive[i] for i, _ in waits])
            key = (ready, late, n)
            if best is None or key < best[0]:
                best = (key, n)
        (ready, _, _), n = best
        name, after, waits, sends, cost, late, work = left.pop(n)
        now = ready + cost + 0.02
        for idx, link, kb, _ in sends:
            lines = {"yp": ("y+", "y-"), "far": ()}.get(link, (link,))
            begin = max([now] + [free.get(line, 0.0) for line in lines])
            if link == "far" and kb < 100:
                begin = max(now, min(free.get("y+", 0.0), free.get("y-", 0.0)))
            if link == "c":
                busy = finish = begin + kb / 200.0
            else:
                finish = begin + kb / rate
                busy = max(finish, begin + kb / (2 * rate) + hop)
            for line in lines:
                free[line] = busy
            arrive[idx] = finish + (1.0 if link == "c" else 2 * hop if link == "far" else hop)
        done.add(name)
        order.append(name)
        if report is not None:
            report.append((name, now))
    return order


def kernel(
    tok_hbm,
    wq_hbm,
    wk_hbm,
    wv_hbm,
    wot_hbm,
    cos_ref,
    sin_ref,
    start_ref,
    gain_ref,
    ogain_ref,
    live_ref,
    out_hbm,
    wbuf,
    obuf,
    xall,
    xstage,
    acc,
    rot,
    vbuf,
    att,
    astage,
    oacc,
    res,
    sqt,
    sqr,
    krow,
    qcol,
    send_sem,
    recv_sem,
    local_sem,
):
    f = lax.axis_index("fsdp")
    t = lax.axis_index("tensor")
    x, yl, z = f // 8, (f // 4) % 2, f % 4
    yh, core = t // 2, t % 2
    y = 2 * yh + yl

    def dev(dx=0, dy=0, dz=0, flip=0):
        ny = (y + dy) % 4
        nf = ((x + dx) % 4) * 8 + (ny % 2) * 4 + (z + dz) % 4
        nc = (core + flip) % 2
        return (nf, (ny // 2) * 2 + nc)

    ypair = ((x * 8 + (1 - yl) * 4 + z), t)
    swap_f = t * 8 + yl * 4 + z
    swap = (swap_f, x)
    sends = []

    def send(src, dst, idx, to):
        copy = pltpu.make_async_remote_copy(
            src_ref=src,
            dst_ref=dst,
            send_sem=send_sem.at[idx],
            recv_sem=recv_sem.at[idx],
            device_id=to,
            device_id_type=MESH,
        )
        copy.start()
        sends.append(copy)

    def recv(dst, idx):
        pltpu.make_async_remote_copy(
            src_ref=dst,
            dst_ref=dst,
            send_sem=send_sem.at[idx],
            recv_sem=recv_sem.at[idx],
            device_id=ypair,
            device_id_type=MESH,
        ).wait_recv()

    events = []

    def event(name, after=(), waits=(), sends=(), cost=0.0, late=0, work=None):
        events.append((name, tuple(after), tuple(waits), tuple(sends), cost, late, work))

    def run():
        for name in plan(events):
            _, _, waits, outs, _, _, work = next(e for e in events if e[0] == name)
            for idx, dst in waits:
                recv(dst(), idx)
            if work is not None:
                work()
            for idx, _, _, what in outs:
                what(idx)

    written = [
        pltpu.make_async_copy(
            res.at[pl.ds(p * HALF, HALF)], out_hbm.at[pl.ds(p * HALF, HALF)], local_sem.at[p]
        )
        for p in range(2)
    ]

    local = [
        pltpu.make_async_copy(wq_hbm, wbuf.at[x, yl, z, :, pl.ds(0, QW)], local_sem.at[0]),
        pltpu.make_async_copy(wk_hbm, wbuf.at[x, yl, z, :, pl.ds(QW, 128)], local_sem.at[1]),
        pltpu.make_async_copy(wv_hbm, wbuf.at[x, yl, z, :, pl.ds(QW + 128, 128)], local_sem.at[2]),
        pltpu.make_async_copy(tok_hbm, xall.at[t], local_sem.at[3]),
    ]
    for copy in local:
        copy.start()

    barrier = pltpu.get_barrier_semaphore()
    partners = [
        dev(dx=1), dev(dx=3), dev(dz=1), dev(dz=3), dev(dy=1), dev(dy=3),
        dev(flip=1), dev(dy=2), dev(dy=2, flip=1),
    ]
    for to in partners:
        pl.semaphore_signal(barrier, inc=1, device_id=to, device_id_type=MESH)

    @pl.when(x != t)
    def _():
        pl.semaphore_signal(barrier, inc=1, device_id=swap, device_id_type=MESH)

    pl.semaphore_wait(barrier, len(partners) + jnp.where(x != t, 1, 0))

    def gather(tag, buf, base, kb, start, start_y, paired):
        order = (0, 3, 1, 2)

        def slot(color, da, yy, db):
            dx, dz = (da, db) if color == 0 else (db, da)
            return buf.at[(x + dx) % 4, yy, (z + dz) % 4, pl.ds(color * 80, 80)]

        def pair(color, da, db):
            dx, dz = (da, db) if color == 0 else (db, da)
            return buf.at[(x + dx) % 4, :, (z + dz) % 4, pl.ds(color * 80, 80)]

        def out(color, stage, sign, k, ref, units=1):
            along_x = (stage == 0) == (color == 0)
            d = sign % 4
            to = dev(dx=d) if along_x else dev(dz=d)
            link = ("x" if along_x else "z") + ("+" if sign > 0 else "-")
            return (base + 24 * color + k, link, units * kb, lambda idx: send(ref(), ref(), idx, to))

        def second(c, k):
            da = order[k]
            return [
                out(c, 1, 1, 6 + 4 * k, lambda: pair(c, da, 0), 2),
                out(c, 1, -1, 7 + 4 * k, lambda: pair(c, da, 0), 2),
            ]

        def half(c, yy):
            return buf.at[x, yy, z, pl.ds(c * 80, 80)]

        for c in range(2):
            event(
                f"{tag}y{c}", start_y,
                sends=[(base + 48 + c, "yp", kb, lambda idx, c=c: send(half(c, yl), half(c, yl), idx, ypair))],
            )
        for stage in range(2):
            for c in range(2):
                k = 0 if stage == 0 else 6
                own = functools.partial(half, c, yl)
                if not paired:
                    event(
                        f"{tag}0{stage}{c}", start,
                        sends=[out(c, stage, 1, k, own), out(c, stage, -1, k + 1, own)],
                    )
        for c in range(2):
            sem = base + 24 * c
            other = functools.partial(half, c, 1 - yl)
            both = functools.partial(pair, c, 0, 0)
            if paired:
                first = [out(c, 0, 1, 0, both, 2), out(c, 0, -1, 1, both, 2)] + second(c, 0)
                left0 = [(sem, lambda c=c: pair(c, 3, 0))]
                right0 = [(sem + 1, lambda c=c: pair(c, 1, 0))]
            else:
                first = [
                    out(c, 0, 1, 2, other), out(c, 0, -1, 3, other),
                    out(c, 1, 1, 22, other), out(c, 1, -1, 23, other),
                ]
                left0 = [(sem, lambda c=c: slot(c, 3, yl, 0)), (sem + 2, lambda c=c: slot(c, 3, 1 - yl, 0))]
                right0 = [(sem + 1, lambda c=c: slot(c, 1, yl, 0)), (sem + 3, lambda c=c: slot(c, 1, 1 - yl, 0))]
            event(f"{tag}1{c}", start, waits=[(base + 48 + c, other)], sends=first)
            event(
                f"{tag}2l{c}", waits=left0,
                sends=[out(c, 0, 1, 4, lambda c=c: slot(c, 3, 0, 0))] + second(c, 1),
            )
            event(
                f"{tag}2r{c}", waits=right0,
                sends=[out(c, 0, -1, 5, lambda c=c: slot(c, 1, 1, 0))] + second(c, 2),
            )
            event(
                f"{tag}3{c}",
                waits=[(sem + 4, lambda c=c: slot(c, 2, 0, 0)), (sem + 5, lambda c=c: slot(c, 2, 1, 0))],
                sends=second(c, 3),
            )
            for k in range(4):
                da = order[k]
                near_l = functools.partial(pair, c, da, 3)
                near_r = functools.partial(pair, c, da, 1)
                far = functools.partial(pair, c, da, 2)
                left = [(sem + 6 + 4 * k, near_l)]
                right = [(sem + 7 + 4 * k, near_r)]
                if k == 0 and not paired:
                    left = [
                        (sem + 6, lambda c=c: slot(c, 0, yl, 3)), (sem + 22, lambda c=c: slot(c, 0, 1 - yl, 3)),
                    ]
                    right = [
                        (sem + 7, lambda c=c: slot(c, 0, yl, 1)), (sem + 23, lambda c=c: slot(c, 0, 1 - yl, 1)),
                    ]
                on_l = [out(c, 1, 1, 8 + 4 * k, lambda c=c, da=da: slot(c, da, 0, 3))]
                on_r = [out(c, 1, -1, 9 + 4 * k, lambda c=c, da=da: slot(c, da, 1, 1))]
                end = [
                    (sem + 8 + 4 * k, lambda c=c, da=da: slot(c, da, 0, 2)),
                    (sem + 9 + 4 * k, lambda c=c, da=da: slot(c, da, 1, 2)),
                ]
                if k == 0:
                    on_l, on_r, end = [out(c, 1, 1, 8, near_l, 2)], [], [(sem + 8, far)]
                if k == 1:
                    on_l, on_r, end = [], [out(c, 1, -1, 13, near_r, 2)], [(sem + 13, far)]
                event(f"{tag}4l{c}{k}", waits=left, sends=on_l)
                event(f"{tag}4r{c}{k}", waits=right, sends=on_r)
                event(f"{tag}5{c}{k}", waits=end)

    def plane(tag, dx):
        k = (0, 3, 1, 2).index(dx)
        need = [f"{tag}4l0{k}", f"{tag}4r0{k}", f"{tag}50{k}", f"{tag}2l0", f"{tag}2r0", f"{tag}30"]
        if dx == 0:
            need += [f"{tag}11", f"{tag}2l1", f"{tag}2r1", f"{tag}31"]
        else:
            need += [f"{tag}" + {3: "4l1", 1: "4r1", 2: "51"}[dx] + f"{n}" for n in range(4)]
        return need + [f"{tag}10", f"{tag}11"]

    def spread(tag, buf, stage, base, chunk, i, kb, after, src=None):
        rows = pl.ds(i * chunk, chunk)
        held = stage.at[i % 2, pl.ds((i // 2) * chunk, chunk)]
        own = buf.at[t, rows] if src is None else src.at[rows]
        d, back, link = (1, 3, "y+") if i % 2 == 0 else (3, 1, "y-")
        came = (((y + back) % 4) // 2) * 2 + core
        far = (t + 2) % 4
        sib = (core + 1) % 2
        base = base + 4 * i
        event(
            f"{tag}o{i}", after,
            sends=[
                (base, link, kb, lambda idx: send(own, held, idx, dev(dy=d))),
                (base + 1, "c", kb, lambda idx: send(own, buf.at[t, rows], idx, dev(flip=1))),
            ],
        )
        event(
            f"{tag}r{i}", waits=[(base, lambda: held)],
            sends=[(base + 2, link, kb, lambda idx: send(held, buf.at[came, rows], idx, dev(dy=d)))],
        )
        event(
            f"{tag}i{i}", waits=[(base + 2, lambda: buf.at[far, rows])],
            sends=[(base + 3, "c", kb, lambda idx: send(buf.at[far, rows], buf.at[far, rows], idx, dev(flip=1)))],
        )
        event(
            f"{tag}d{i}",
            waits=[
                (base + 1, lambda: buf.at[yh * 2 + sib, rows]),
                (base + 3, lambda: buf.at[(1 - yh) * 2 + sib, rows]),
            ],
        )

    def exchange(k, p, after):
        cols = pl.ds(p * HALF, HALF)
        outs = []
        for n, to in enumerate((dev(flip=1), dev(dy=2), dev(dy=2, flip=1))):
            outs.append((
                SEM_S + 6 * k + 3 * p + n, "c" if n == 0 else "far", 12,
                lambda idx, n=n, to=to: send(sqt.at[k, p, pl.ds(0, 8)], sqr.at[k, p, n], idx, to),
            ))
        event(f"x{k}{p}", after, sends=outs)

    def exchanged(k, p):
        return [(SEM_S + 6 * k + 3 * p + n, lambda n=n: sqr.at[k, p, n]) for n in range(3)]

    def total(k, p):
        return sqt[k, p, pl.ds(0, 8)] + sqr[k, p, 0] + sqr[k, p, 1] + sqr[k, p, 2]

    def qkv(row, size, dx, first):
        j = (x + dx) % 4
        rows = pl.ds(row, size)
        part = jnp.dot(
            xall[j, rows], wbuf[j].reshape(TCOL, QKV), preferred_element_type=jnp.float32
        )
        if first:
            acc[rows] = part
        else:
            acc[rows] += part

    lane = lax.broadcasted_iota(jnp.int32, (HALF, 128), 1)

    def sums(p):
        rows = pl.ds(p * HALF, HALF)
        q = acc[rows, pl.ds(0, QW)]
        k = acc[rows, pl.ds(QW, 128)]
        qs = jnp.sum(q * q, axis=1, keepdims=True)
        ks = jnp.sum(k * k, axis=1, keepdims=True)
        both = jnp.where(lane < 4, qs, ks)
        sqt[0, p] = both.T

    def rotate(p):
        rows = pl.ds(p * HALF, HALF)
        for h in range(6):
            cols = pl.ds(h * 128, 128)
            u = acc[rows, cols] * gain_ref[:, cols]
            r = u * cos_ref[rows] + pltpu.roll(u, 64, 1) * sin_ref[rows]
            rot[h, rows] = r.astype(jnp.bfloat16)
        vbuf[rows] = acc[rows, pl.ds(QW + 128, 128)].astype(jnp.bfloat16)

    def scales(p):
        sq = total(0, p)
        res_q = lax.rsqrt(sq[0:4] / (HEADS * HEAD_DIM) + EPS) * (1.0 / math.sqrt(HEAD_DIM))
        res_k = lax.rsqrt(sq[4:8] / (KV_HEADS * HEAD_DIM) + EPS)
        both = jnp.concatenate([res_q, res_k], axis=0)
        krow[p] = both
        qcol[p] = jnp.concatenate([both] * 16, axis=0).T

    def attend(p, b):
        rows = pl.ds(p * HALF + b * 128, 128)
        width = (b + 1) * 128
        seen = pl.ds(p * HALF, width)
        first = start_ref[rows] - p * HALF
        col = lax.broadcasted_iota(jnp.int32, (128, width), 1)
        row = lax.broadcasted_iota(jnp.int32, (128, width), 0) + b * 128
        bias = jnp.where((col >= first) & (col <= row), 0.0, -1e30).astype(jnp.float32)
        scale = qcol[p, pl.ds(b * 128, 128), 0:1] * krow[p, 4:5, 0:width]
        s = lax.dot_general(
            rot[0:5, rows].reshape(QW, 128), rot[5, seen], (((1,), (1,)), ((), ())),
            preferred_element_type=jnp.float32,
        ).reshape(5, 128, width)
        s = s * scale[None] + bias[None]
        e = jnp.exp(s - jnp.max(s, axis=2, keepdims=True))
        inv = 1.0 / jnp.sum(e, axis=2, keepdims=True)
        o = jnp.dot(
            e.astype(jnp.bfloat16).reshape(QW, width), vbuf[seen], preferred_element_type=jnp.float32
        ).reshape(5, 128, 128)
        o = (o * inv).astype(jnp.bfloat16)
        for h in range(5):
            att[t, rows, pl.ds(h * 128, 128)] = o[h]

    def project(p, dx, first):
        j = (x + dx) % 4
        rows = pl.ds(p * HALF, HALF)
        part = lax.dot_general(
            att[j, rows],
            obuf[j].reshape(TCOL, QW),
            (((1,), (1,)), ((), ())),
            preferred_element_type=jnp.float32,
        )
        if first:
            oacc[rows] = part
        else:
            oacc[rows] += part

    def out_sums(p):
        rows = pl.ds(p * HALF, HALF)
        o = oacc[rows]
        sqt[1, p] = jnp.broadcast_to(jnp.sum(o * o, axis=1, keepdims=True), (HALF, 128)).T

    def finish(p):
        sums_out = jnp.concatenate([total(1, p)] * 16, axis=0).T
        rows = pl.ds(p * HALF, HALF)
        scale = lax.rsqrt(sums_out[:, 0:1] / D + EPS)
        r = xall[t, rows].astype(jnp.float32) + oacc[rows] * scale * ogain_ref[...]
        row = lax.broadcasted_iota(jnp.int32, (HALF, TCOL), 0) + p * HALF
        res[rows] = jnp.where(row < live_ref[0], r, 0.0).astype(jnp.bfloat16)
        written[p].start()

    for copy in local[:3]:
        copy.wait()

    own_o = obuf.at[x, yl, z]

    def swap_out():
        @pl.when(x != t)
        def _():
            copy = pltpu.make_async_remote_copy(
                src_ref=wot_hbm, dst_ref=obuf.at[t, yl, z], send_sem=send_sem.at[SEM_P],
                recv_sem=recv_sem.at[SEM_P], device_id=swap, device_id_type=MESH,
            )
            copy.start()

        @pl.when(x == t)
        def _():
            copy = pltpu.make_async_copy(wot_hbm, own_o, local_sem.at[4])
            copy.start()

    def swap_in():
        @pl.when(x != t)
        def _():
            copy = pltpu.make_async_remote_copy(
                src_ref=wot_hbm, dst_ref=own_o, send_sem=send_sem.at[SEM_P],
                recv_sem=recv_sem.at[SEM_P], device_id=swap, device_id_type=MESH,
            )
            copy.wait()

        @pl.when(x == t)
        def _():
            copy = pltpu.make_async_copy(wot_hbm, own_o, local_sem.at[4])
            copy.wait()

    w_sends = [f"w4{s}{c}{k}" for s in "lr" for c in range(2) for k in range(4)]
    gather("w", wbuf, SEM_W, 143.4, (), (), False)
    event("swap", ("w010", "w011"), sends=[(SEM_P, "far", 205, lambda idx: swap_out())])
    for i in range(TOK_N):
        spread("t", xall, xstage, SEM_T, TOK_CHUNK, i, 163.8, ("wy0", "wy1", "w010", "w011"), tok_hbm)
    event("swapped", ("swap", "tr5"), cost=0.1, work=swap_in)
    gather("o", obuf, SEM_O, 102.4, ["swapped"] + w_sends, ["swapped"], True)
    event("own", work=local[3].wait)

    for p in range(2):
        blocks = [(0, HALF)] if p == 0 else [(HALF, HALF // 2), (HALF + HALF // 2, HALF // 2)]
        for m, (row, size) in enumerate(blocks):
            chunks = range(row // TOK_CHUNK, (row + size) // TOK_CHUNK)
            rows_in = ["own"] + [f"t{s}{i}" for s in "rid" for i in chunks]
            for n, dx in enumerate((0, 3, 1, 2)):
                event(
                    f"q{p}{m}{n}", rows_in + plane("w", dx) + ([f"q{p}{m}{n - 1}"] if n else []),
                    cost=1.25 * size / HALF, late=1, work=functools.partial(qkv, row, size, dx, n == 0),
                )
        event(f"sum{p}", [f"q{p}{m}3" for m in range(len(blocks))], cost=0.2, late=1, work=functools.partial(sums, p))
        exchange(0, p, [f"sum{p}"])
        event(f"rot{p}", [f"x0{p}"], cost=0.4, late=1, work=functools.partial(rotate, p))
        event(f"scale{p}", [f"rot{p}"], waits=exchanged(0, p), cost=0.2, late=1, work=functools.partial(scales, p))
    half_a = ATT_N // 2
    for i in range(ATT_N):
        p, b = i // 3, i % 3
        prev = f"att{i - 1}" if b else f"scale{p}"
        event(f"att{i}", (prev,), cost=0.6 + 0.4 * b, late=0.5 + p, work=functools.partial(attend, p, b))
        spread("a", att, astage, SEM_A, ATT_CHUNK, i, 163.8, (f"att{i}",))
    for p in range(2):
        rows_in = [f"a{s}{p * half_a + i}" for s in "orid" for i in range(half_a)]
        for n, dx in enumerate((0, 3, 1, 2)):
            event(
                f"p{p}{n}", rows_in + plane("o", dx) + ([f"p{p}{n - 1}"] if n else []),
                cost=0.7, late=1, work=functools.partial(project, p, dx, n == 0),
            )
        event(f"osum{p}", [f"p{p}3"], cost=0.2, late=1, work=functools.partial(out_sums, p))
        exchange(1, p, [f"osum{p}"])
        event(f"end{p}", (f"x1{p}",), waits=exchanged(1, p), cost=1.2, late=1, work=functools.partial(finish, p))
    run()
    for copy in written:
        copy.wait()
    for copy in sends:
        copy.wait_send()


def body(
    tokens, live_rows, first_row, w_query, w_key, w_value, w_out, query_gain, key_gain, out_gain
):
    half = HEAD_DIM // 2
    freqs = jnp.power(ROPE_BASE, -(jnp.arange(half, dtype=jnp.float32) * 2.0 / HEAD_DIM))
    positions = (jnp.arange(CAP, dtype=jnp.int32) - first_row).astype(jnp.float32)
    angle = positions[:, None] * freqs[None, :]
    cosine, sine = jnp.cos(angle), jnp.sin(angle)
    cos = jnp.concatenate([cosine, cosine], axis=1)
    sin = jnp.concatenate([-sine, sine], axis=1)
    gains = jnp.concatenate([query_gain, key_gain])[None, :]
    hbm = pl.BlockSpec(memory_space=pl.ANY)
    vmem = pl.BlockSpec(memory_space=pltpu.VMEM)
    smem = pl.BlockSpec(memory_space=pltpu.SMEM)
    bf, fl = jnp.bfloat16, jnp.float32
    return pl.pallas_call(
        kernel,
        out_shape=jax.ShapeDtypeStruct((CAP, TCOL), bf),
        in_specs=[hbm] * 5 + [vmem] * 5 + [smem],
        out_specs=hbm,
        scratch_shapes=[
            pltpu.VMEM((4, 2, 4, SHARD, QKV), bf),
            pltpu.VMEM((4, 2, 4, SHARD, QW), bf),
            pltpu.VMEM((4, CAP, TCOL), bf),
            pltpu.VMEM((2, HALF, TCOL), bf),
            pltpu.VMEM((CAP, QKV), fl),
            pltpu.VMEM((6, CAP, 128), bf),
            pltpu.VMEM((CAP, 128), bf),
            pltpu.VMEM((4, CAP, QW), bf),
            pltpu.VMEM((2, HALF, QW), bf),
            pltpu.VMEM((CAP, TCOL), fl),
            pltpu.VMEM((CAP, TCOL), bf),
            pltpu.VMEM((2, 2, 128, HALF), fl),
            pltpu.VMEM((2, 2, 3, 8, HALF), fl),
            pltpu.VMEM((2, 8, HALF), fl),
            pltpu.VMEM((2, HALF, 128), fl),
            pltpu.SemaphoreType.DMA((SEM_N,)),
            pltpu.SemaphoreType.DMA((SEM_N,)),
            pltpu.SemaphoreType.DMA((5,)),
        ],
        compiler_params=pltpu.CompilerParams(
            collective_id=0, has_side_effects=True, vmem_limit_bytes=60 * 1024 * 1024
        ),
    )(
        tokens,
        w_query,
        w_key,
        w_value,
        w_out.T,
        cos,
        sin,
        first_row[:, None],
        gains,
        out_gain[None, :],
        live_rows,
    )


def solution(mesh):
    in_specs = (
        P("fsdp", "tensor"),
        P("fsdp"),
        P("fsdp"),
        P("fsdp", "tensor"),
        P("fsdp", "tensor"),
        P("fsdp", "tensor"),
        P("tensor", "fsdp"),
        P("tensor"),
        P("tensor"),
        P("tensor"),
    )
    return jax.shard_map(
        body, mesh=mesh, in_specs=in_specs, out_specs=P("fsdp", "tensor"), check_vma=False
    )
```

```python
import functools
import math

import jax
import jax.numpy as jnp
from jax import lax
from jax.experimental import pallas as pl
from jax.experimental.pallas import tpu as pltpu
from jax.sharding import PartitionSpec as P

D = 5120
HEADS = 20
KV_HEADS = 4
HEAD_DIM = 128
CAP = 768
HALF = 384
EPS = 1e-06
ROPE_BASE = 500000.0
SHARD = 160
QKV = 896
QW = 640
TCOL = 1280
MESH = pl.DeviceIdType.MESH

TOK_CHUNK = 64
TOK_N = CAP // TOK_CHUNK
ATT_CHUNK = 128
ATT_N = CAP // ATT_CHUNK

AG_SEMS = 2 * 24 + 2
SEM_W = 0
SEM_O = SEM_W + AG_SEMS
SEM_T = SEM_O + AG_SEMS
SEM_A = SEM_T + 4 * TOK_N
SEM_S = SEM_A + 4 * ATT_N
SEM_P = SEM_S + 12
SEM_N = SEM_P + 1


def plan(events, rate=45.0, hop=1.8, report=None):
    now, done, arrive, free, order = 0.0, set(), {}, {}, []
    left = list(events)
    while left:
        best = None
        for n, (name, after, waits, sends, cost, late, work) in enumerate(left):
            if any(a not in done for a in after) or any(i not in arrive for i, _ in waits):
                continue
            ready = max([now] + [arrive[i] for i, _ in waits])
            key = (ready, late, n)
            if best is None or key < best[0]:
                best = (key, n)
        (ready, _, _), n = best
        name, after, waits, sends, cost, late, work = left.pop(n)
        now = ready + cost + 0.02
        for idx, link, kb, _ in sends:
            lines = {"yp": ("y+", "y-"), "far": ()}.get(link, (link,))
            begin = max([now] + [free.get(line, 0.0) for line in lines])
            if link == "far" and kb < 100:
                begin = max(now, min(free.get("y+", 0.0), free.get("y-", 0.0)))
            if link == "c":
                busy = finish = begin + kb / 200.0
            else:
                finish = begin + kb / rate
                busy = max(finish, begin + kb / (2 * rate) + hop)
            for line in lines:
                free[line] = busy
            arrive[idx] = finish + (1.0 if link == "c" else 2 * hop if link == "far" else hop)
        done.add(name)
        order.append(name)
        if report is not None:
            report.append((name, now))
    return order


def kernel(
    tok_hbm,
    wq_hbm,
    wk_hbm,
    wv_hbm,
    wot_hbm,
    first_hbm,
    qgain_hbm,
    kgain_hbm,
    ogain_hbm,
    live_ref,
    out_hbm,
    wbuf,
    obuf,
    xall,
    xstage,
    acc,
    rot,
    vbuf,
    att,
    astage,
    oacc,
    res,
    sqt,
    sqr,
    krow,
    qcol,
    cos_ref,
    sin_ref,
    start_ref,
    first_v,
    qgain_v,
    kgain_v,
    ogain_v,
    send_sem,
    recv_sem,
    local_sem,
):
    f = lax.axis_index("fsdp")
    t = lax.axis_index("tensor")
    x, yl, z = f // 8, (f // 4) % 2, f % 4
    yh, core = t // 2, t % 2
    y = 2 * yh + yl

    def dev(dx=0, dy=0, dz=0, flip=0):
        ny = (y + dy) % 4
        nf = ((x + dx) % 4) * 8 + (ny % 2) * 4 + (z + dz) % 4
        nc = (core + flip) % 2
        return (nf, (ny // 2) * 2 + nc)

    ypair = ((x * 8 + (1 - yl) * 4 + z), t)
    swap_f = t * 8 + yl * 4 + z
    swap = (swap_f, x)
    sends = []

    def send(src, dst, idx, to):
        copy = pltpu.make_async_remote_copy(
            src_ref=src,
            dst_ref=dst,
            send_sem=send_sem.at[idx],
            recv_sem=recv_sem.at[idx],
            device_id=to,
            device_id_type=MESH,
        )
        copy.start()
        sends.append(copy)

    def recv(dst, idx):
        pltpu.make_async_remote_copy(
            src_ref=dst,
            dst_ref=dst,
            send_sem=send_sem.at[idx],
            recv_sem=recv_sem.at[idx],
            device_id=ypair,
            device_id_type=MESH,
        ).wait_recv()

    events = []

    def event(name, after=(), waits=(), sends=(), cost=0.0, late=0, work=None):
        events.append((name, tuple(after), tuple(waits), tuple(sends), cost, late, work))

    def run():
        for name in plan(events):
            _, _, waits, outs, _, _, work = next(e for e in events if e[0] == name)
            for idx, dst in waits:
                recv(dst(), idx)
            if work is not None:
                work()
            for idx, _, _, what in outs:
                what(idx)

    written = [
        pltpu.make_async_copy(
            res.at[pl.ds(p * HALF, HALF)], out_hbm.at[pl.ds(p * HALF, HALF)], local_sem.at[p]
        )
        for p in range(2)
    ]

    local = [
        pltpu.make_async_copy(wq_hbm, wbuf.at[x, yl, z, :, pl.ds(0, QW)], local_sem.at[0]),
        pltpu.make_async_copy(wk_hbm, wbuf.at[x, yl, z, :, pl.ds(QW, 128)], local_sem.at[1]),
        pltpu.make_async_copy(wv_hbm, wbuf.at[x, yl, z, :, pl.ds(QW + 128, 128)], local_sem.at[2]),
        pltpu.make_async_copy(tok_hbm, xall.at[t], local_sem.at[3]),
        pltpu.make_async_copy(first_hbm, first_v, local_sem.at[5]),
        pltpu.make_async_copy(qgain_hbm, qgain_v, local_sem.at[6]),
        pltpu.make_async_copy(kgain_hbm, kgain_v, local_sem.at[7]),
        pltpu.make_async_copy(ogain_hbm, ogain_v, local_sem.at[8]),
    ]
    for copy in local:
        copy.start()

    barrier = pltpu.get_barrier_semaphore()
    partners = [
        dev(dx=1), dev(dx=3), dev(dz=1), dev(dz=3), dev(dy=1), dev(dy=3),
        dev(flip=1), dev(dy=2), dev(dy=2, flip=1),
    ]
    for to in partners:
        pl.semaphore_signal(barrier, inc=1, device_id=to, device_id_type=MESH)

    @pl.when(x != t)
    def _():
        pl.semaphore_signal(barrier, inc=1, device_id=swap, device_id_type=MESH)

    pl.semaphore_wait(barrier, len(partners) + jnp.where(x != t, 1, 0))

    def gather(tag, buf, base, kb, start, start_y, paired):
        order = (0, 3, 1, 2)

        def slot(color, da, yy, db):
            dx, dz = (da, db) if color == 0 else (db, da)
            return buf.at[(x + dx) % 4, yy, (z + dz) % 4, pl.ds(color * 80, 80)]

        def pair(color, da, db):
            dx, dz = (da, db) if color == 0 else (db, da)
            return buf.at[(x + dx) % 4, :, (z + dz) % 4, pl.ds(color * 80, 80)]

        def out(color, stage, sign, k, ref, units=1):
            along_x = (stage == 0) == (color == 0)
            d = sign % 4
            to = dev(dx=d) if along_x else dev(dz=d)
            link = ("x" if along_x else "z") + ("+" if sign > 0 else "-")
            return (base + 24 * color + k, link, units * kb, lambda idx: send(ref(), ref(), idx, to))

        def second(c, k):
            da = order[k]
            return [
                out(c, 1, 1, 6 + 4 * k, lambda: pair(c, da, 0), 2),
                out(c, 1, -1, 7 + 4 * k, lambda: pair(c, da, 0), 2),
            ]

        def half(c, yy):
            return buf.at[x, yy, z, pl.ds(c * 80, 80)]

        for c in range(2):
            event(
                f"{tag}y{c}", start_y,
                sends=[(base + 48 + c, "yp", kb, lambda idx, c=c: send(half(c, yl), half(c, yl), idx, ypair))],
            )
        for stage in range(2):
            for c in range(2):
                k = 0 if stage == 0 else 6
                own = functools.partial(half, c, yl)
                if not paired:
                    event(
                        f"{tag}0{stage}{c}", start,
                        sends=[out(c, stage, 1, k, own), out(c, stage, -1, k + 1, own)],
                    )
        for c in range(2):
            sem = base + 24 * c
            other = functools.partial(half, c, 1 - yl)
            both = functools.partial(pair, c, 0, 0)
            if paired:
                first = [out(c, 0, 1, 0, both, 2), out(c, 0, -1, 1, both, 2)] + second(c, 0)
                left0 = [(sem, lambda c=c: pair(c, 3, 0))]
                right0 = [(sem + 1, lambda c=c: pair(c, 1, 0))]
            else:
                first = [
                    out(c, 0, 1, 2, other), out(c, 0, -1, 3, other),
                    out(c, 1, 1, 22, other), out(c, 1, -1, 23, other),
                ]
                left0 = [(sem, lambda c=c: slot(c, 3, yl, 0)), (sem + 2, lambda c=c: slot(c, 3, 1 - yl, 0))]
                right0 = [(sem + 1, lambda c=c: slot(c, 1, yl, 0)), (sem + 3, lambda c=c: slot(c, 1, 1 - yl, 0))]
            event(f"{tag}1{c}", start, waits=[(base + 48 + c, other)], sends=first)
            event(
                f"{tag}2l{c}", waits=left0,
                sends=[out(c, 0, 1, 4, lambda c=c: slot(c, 3, 0, 0))] + second(c, 1),
            )
            event(
                f"{tag}2r{c}", waits=right0,
                sends=[out(c, 0, -1, 5, lambda c=c: slot(c, 1, 1, 0))] + second(c, 2),
            )
            event(
                f"{tag}3{c}",
                waits=[(sem + 4, lambda c=c: slot(c, 2, 0, 0)), (sem + 5, lambda c=c: slot(c, 2, 1, 0))],
                sends=second(c, 3),
            )
            for k in range(4):
                da = order[k]
                near_l = functools.partial(pair, c, da, 3)
                near_r = functools.partial(pair, c, da, 1)
                far = functools.partial(pair, c, da, 2)
                left = [(sem + 6 + 4 * k, near_l)]
                right = [(sem + 7 + 4 * k, near_r)]
                if k == 0 and not paired:
                    left = [
                        (sem + 6, lambda c=c: slot(c, 0, yl, 3)), (sem + 22, lambda c=c: slot(c, 0, 1 - yl, 3)),
                    ]
                    right = [
                        (sem + 7, lambda c=c: slot(c, 0, yl, 1)), (sem + 23, lambda c=c: slot(c, 0, 1 - yl, 1)),
                    ]
                on_l = [out(c, 1, 1, 8 + 4 * k, lambda c=c, da=da: slot(c, da, 0, 3))]
                on_r = [out(c, 1, -1, 9 + 4 * k, lambda c=c, da=da: slot(c, da, 1, 1))]
                end = [
                    (sem + 8 + 4 * k, lambda c=c, da=da: slot(c, da, 0, 2)),
                    (sem + 9 + 4 * k, lambda c=c, da=da: slot(c, da, 1, 2)),
                ]
                if k == 0:
                    on_l, on_r, end = [out(c, 1, 1, 8, near_l, 2)], [], [(sem + 8, far)]
                if k == 1:
                    on_l, on_r, end = [], [out(c, 1, -1, 13, near_r, 2)], [(sem + 13, far)]
                event(f"{tag}4l{c}{k}", waits=left, sends=on_l)
                event(f"{tag}4r{c}{k}", waits=right, sends=on_r)
                event(f"{tag}5{c}{k}", waits=end)

    def plane(tag, dx):
        k = (0, 3, 1, 2).index(dx)
        need = [f"{tag}4l0{k}", f"{tag}4r0{k}", f"{tag}50{k}", f"{tag}2l0", f"{tag}2r0", f"{tag}30"]
        if dx == 0:
            need += [f"{tag}11", f"{tag}2l1", f"{tag}2r1", f"{tag}31"]
        else:
            need += [f"{tag}" + {3: "4l1", 1: "4r1", 2: "51"}[dx] + f"{n}" for n in range(4)]
        return need + [f"{tag}10", f"{tag}11"]

    def spread(tag, buf, stage, base, chunk, i, kb, after, src=None):
        rows = pl.ds(i * chunk, chunk)
        held = stage.at[i % 2, pl.ds((i // 2) * chunk, chunk)]
        own = buf.at[t, rows] if src is None else src.at[rows]
        d, back, link = (1, 3, "y+") if i % 2 == 0 else (3, 1, "y-")
        came = (((y + back) % 4) // 2) * 2 + core
        far = (t + 2) % 4
        sib = (core + 1) % 2
        base = base + 4 * i
        event(
            f"{tag}o{i}", after,
            sends=[
                (base, link, kb, lambda idx: send(own, held, idx, dev(dy=d))),
                (base + 1, "c", kb, lambda idx: send(own, buf.at[t, rows], idx, dev(flip=1))),
            ],
        )
        event(
            f"{tag}r{i}", waits=[(base, lambda: held)],
            sends=[(base + 2, link, kb, lambda idx: send(held, buf.at[came, rows], idx, dev(dy=d)))],
        )
        event(
            f"{tag}i{i}", waits=[(base + 2, lambda: buf.at[far, rows])],
            sends=[(base + 3, "c", kb, lambda idx: send(buf.at[far, rows], buf.at[far, rows], idx, dev(flip=1)))],
        )
        event(
            f"{tag}d{i}",
            waits=[
                (base + 1, lambda: buf.at[yh * 2 + sib, rows]),
                (base + 3, lambda: buf.at[(1 - yh) * 2 + sib, rows]),
            ],
        )

    def exchange(k, p, after):
        cols = pl.ds(p * HALF, HALF)
        outs = []
        for n, to in enumerate((dev(flip=1), dev(dy=2), dev(dy=2, flip=1))):
            outs.append((
                SEM_S + 6 * k + 3 * p + n, "c" if n == 0 else "far", 12,
                lambda idx, n=n, to=to: send(sqt.at[k, p, pl.ds(0, 8)], sqr.at[k, p, n], idx, to),
            ))
        event(f"x{k}{p}", after, sends=outs)

    def exchanged(k, p):
        return [(SEM_S + 6 * k + 3 * p + n, lambda n=n: sqr.at[k, p, n]) for n in range(3)]

    def total(k, p):
        return sqt[k, p, pl.ds(0, 8)] + sqr[k, p, 0] + sqr[k, p, 1] + sqr[k, p, 2]

    def qkv(row, size, dx, first):
        j = (x + dx) % 4
        rows = pl.ds(row, size)
        part = jnp.dot(
            xall[j, rows], wbuf[j].reshape(TCOL, QKV), preferred_element_type=jnp.float32
        )
        if first:
            acc[rows] = part
        else:
            acc[rows] += part

    lane = lax.broadcasted_iota(jnp.int32, (HALF, 128), 1)

    def sums(p):
        rows = pl.ds(p * HALF, HALF)
        q = acc[rows, pl.ds(0, QW)]
        k = acc[rows, pl.ds(QW, 128)]
        qs = jnp.sum(q * q, axis=1, keepdims=True)
        ks = jnp.sum(k * k, axis=1, keepdims=True)
        both = jnp.where(lane < 4, qs, ks)
        sqt[0, p] = both.T

    def tables():
        for copy in local[4:]:
            copy.wait()
        first = jnp.broadcast_to(first_v[...].reshape(1, CAP), (128, CAP)).astype(jnp.float32).T
        wide = lax.broadcasted_iota(jnp.int32, (CAP, 128), 1)
        local_row = lax.broadcasted_iota(jnp.int32, (CAP, 128), 0).astype(jnp.float32)
        freqs = jnp.power(ROPE_BASE, -((wide % 64).astype(jnp.float32) * 2.0 / HEAD_DIM))
        angle = (local_row - first) * freqs
        sine = jnp.sin(angle)
        cos_ref[...] = jnp.cos(angle)
        sin_ref[...] = jnp.where(wide < 64, -sine, sine)
        start_ref[...] = first.astype(jnp.int32)

    def rotate(p):
        rows = pl.ds(p * HALF, HALF)
        gains = jnp.concatenate([qgain_v[...].reshape(1, QW), kgain_v[...].reshape(1, 128)], axis=1)
        for h in range(6):
            cols = pl.ds(h * 128, 128)
            u = acc[rows, cols] * gains[:, h * 128 : (h + 1) * 128]
            r = u * cos_ref[rows] + pltpu.roll(u, 64, 1) * sin_ref[rows]
            rot[h, rows] = r.astype(jnp.bfloat16)
        vbuf[rows] = acc[rows, pl.ds(QW + 128, 128)].astype(jnp.bfloat16)

    def scales(p):
        sq = total(0, p)
        res_q = lax.rsqrt(sq[0:4] / (HEADS * HEAD_DIM) + EPS) * (1.0 / math.sqrt(HEAD_DIM))
        res_k = lax.rsqrt(sq[4:8] / (KV_HEADS * HEAD_DIM) + EPS)
        both = jnp.concatenate([res_q, res_k], axis=0)
        krow[p] = both
        qcol[p] = jnp.concatenate([both] * 16, axis=0).T

    def attend(p, b):
        rows = pl.ds(p * HALF + b * 128, 128)
        width = (b + 1) * 128
        seen = pl.ds(p * HALF, width)
        first = start_ref[rows, 0:1] - p * HALF
        col = lax.broadcasted_iota(jnp.int32, (128, width), 1)
        row = lax.broadcasted_iota(jnp.int32, (128, width), 0) + b * 128
        bias = jnp.where((col >= first) & (col <= row), 0.0, -1e30).astype(jnp.float32)
        scale = qcol[p, pl.ds(b * 128, 128), 0:1] * krow[p, 4:5, 0:width]
        s = lax.dot_general(
            rot[0:5, rows].reshape(QW, 128), rot[5, seen], (((1,), (1,)), ((), ())),
            preferred_element_type=jnp.float32,
        ).reshape(5, 128, width)
        s = s * scale[None] + bias[None]
        e = jnp.exp(s - jnp.max(s, axis=2, keepdims=True))
        inv = 1.0 / jnp.sum(e, axis=2, keepdims=True)
        o = jnp.dot(
            e.astype(jnp.bfloat16).reshape(QW, width), vbuf[seen], preferred_element_type=jnp.float32
        ).reshape(5, 128, 128)
        o = (o * inv).astype(jnp.bfloat16)
        for h in range(5):
            att[t, rows, pl.ds(h * 128, 128)] = o[h]

    def project(p, dx, first):
        j = (x + dx) % 4
        rows = pl.ds(p * HALF, HALF)
        part = lax.dot_general(
            att[j, rows],
            obuf[j].reshape(TCOL, QW),
            (((1,), (1,)), ((), ())),
            preferred_element_type=jnp.float32,
        )
        if first:
            oacc[rows] = part
        else:
            oacc[rows] += part

    def out_sums(p):
        rows = pl.ds(p * HALF, HALF)
        o = oacc[rows]
        sqt[1, p] = jnp.broadcast_to(jnp.sum(o * o, axis=1, keepdims=True), (HALF, 128)).T

    def finish(p):
        sums_out = jnp.concatenate([total(1, p)] * 16, axis=0).T
        rows = pl.ds(p * HALF, HALF)
        scale = lax.rsqrt(sums_out[:, 0:1] / D + EPS)
        r = xall[t, rows].astype(jnp.float32) + oacc[rows] * scale * ogain_v[...].reshape(1, TCOL)
        row = lax.broadcasted_iota(jnp.int32, (HALF, TCOL), 0) + p * HALF
        res[rows] = jnp.where(row < live_ref[0], r, 0.0).astype(jnp.bfloat16)
        written[p].start()

    for copy in local[:3]:
        copy.wait()

    own_o = obuf.at[x, yl, z]

    def swap_out():
        @pl.when(x != t)
        def _():
            copy = pltpu.make_async_remote_copy(
                src_ref=wot_hbm, dst_ref=obuf.at[t, yl, z], send_sem=send_sem.at[SEM_P],
                recv_sem=recv_sem.at[SEM_P], device_id=swap, device_id_type=MESH,
            )
            copy.start()

        @pl.when(x == t)
        def _():
            copy = pltpu.make_async_copy(wot_hbm, own_o, local_sem.at[4])
            copy.start()

    def swap_in():
        @pl.when(x != t)
        def _():
            copy = pltpu.make_async_remote_copy(
                src_ref=wot_hbm, dst_ref=own_o, send_sem=send_sem.at[SEM_P],
                recv_sem=recv_sem.at[SEM_P], device_id=swap, device_id_type=MESH,
            )
            copy.wait()

        @pl.when(x == t)
        def _():
            copy = pltpu.make_async_copy(wot_hbm, own_o, local_sem.at[4])
            copy.wait()

    w_sends = [f"w4{s}{c}{k}" for s in "lr" for c in range(2) for k in range(4)]
    gather("w", wbuf, SEM_W, 143.4, (), (), False)
    event("swap", ("w010", "w011"), sends=[(SEM_P, "far", 205, lambda idx: swap_out())])
    for i in range(TOK_N):
        spread("t", xall, xstage, SEM_T, TOK_CHUNK, i, 163.8, ("wy0", "wy1", "w010", "w011"), tok_hbm)
    event("swapped", ("swap", "tr5"), cost=0.1, work=swap_in)
    gather("o", obuf, SEM_O, 102.4, ["swapped"] + w_sends, ["swapped"], True)
    event("own", work=local[3].wait)
    event("tables", ["to11"], cost=3.0, late=1, work=tables)

    for p in range(2):
        blocks = [(0, HALF)] if p == 0 else [(HALF, HALF // 2), (HALF + HALF // 2, HALF // 2)]
        for m, (row, size) in enumerate(blocks):
            chunks = range(row // TOK_CHUNK, (row + size) // TOK_CHUNK)
            rows_in = ["own"] + [f"t{s}{i}" for s in "rid" for i in chunks]
            for n, dx in enumerate((0, 3, 1, 2)):
                event(
                    f"q{p}{m}{n}", rows_in + plane("w", dx) + ([f"q{p}{m}{n - 1}"] if n else []),
                    cost=1.25 * size / HALF, late=1, work=functools.partial(qkv, row, size, dx, n == 0),
                )
        event(f"sum{p}", [f"q{p}{m}3" for m in range(len(blocks))], cost=0.2, late=1, work=functools.partial(sums, p))
        exchange(0, p, [f"sum{p}"])
        event(f"rot{p}", [f"x0{p}", "tables"], cost=0.4, late=1, work=functools.partial(rotate, p))
        event(f"scale{p}", [f"rot{p}"], waits=exchanged(0, p), cost=0.2, late=1, work=functools.partial(scales, p))
    half_a = ATT_N // 2
    for i in range(ATT_N):
        p, b = i // 3, i % 3
        prev = f"att{i - 1}" if b else f"scale{p}"
        event(f"att{i}", (prev,), cost=0.6 + 0.4 * b, late=0.5 + p, work=functools.partial(attend, p, b))
        spread("a", att, astage, SEM_A, ATT_CHUNK, i, 163.8, (f"att{i}",))
    for p in range(2):
        rows_in = [f"a{s}{p * half_a + i}" for s in "orid" for i in range(half_a)]
        for n, dx in enumerate((0, 3, 1, 2)):
            event(
                f"p{p}{n}", rows_in + plane("o", dx) + ([f"p{p}{n - 1}"] if n else []),
                cost=0.7, late=1, work=functools.partial(project, p, dx, n == 0),
            )
        event(f"osum{p}", [f"p{p}3"], cost=0.2, late=1, work=functools.partial(out_sums, p))
        exchange(1, p, [f"osum{p}"])
        event(f"end{p}", (f"x1{p}",), waits=exchanged(1, p), cost=1.2, late=1, work=functools.partial(finish, p))
    run()
    for copy in written:
        copy.wait()
    for copy in sends:
        copy.wait_send()


def body(
    tokens, live_rows, first_row, w_query, w_key, w_value, w_out, query_gain, key_gain, out_gain
):
    hbm = pl.BlockSpec(memory_space=pltpu.HBM)
    smem = pl.BlockSpec(memory_space=pltpu.SMEM)
    bf, fl = jnp.bfloat16, jnp.float32
    return pl.pallas_call(
        kernel,
        out_shape=jax.ShapeDtypeStruct((CAP, TCOL), bf),
        in_specs=[hbm] * 9 + [smem],
        out_specs=pl.BlockSpec(memory_space=pl.ANY),
        scratch_shapes=[
            pltpu.VMEM((4, 2, 4, SHARD, QKV), bf),
            pltpu.VMEM((4, 2, 4, SHARD, QW), bf),
            pltpu.VMEM((4, CAP, TCOL), bf),
            pltpu.VMEM((2, HALF, TCOL), bf),
            pltpu.VMEM((CAP, QKV), fl),
            pltpu.VMEM((6, CAP, 128), bf),
            pltpu.VMEM((CAP, 128), bf),
            pltpu.VMEM((4, CAP, QW), bf),
            pltpu.VMEM((2, HALF, QW), bf),
            pltpu.VMEM((CAP, TCOL), fl),
            pltpu.VMEM((CAP, TCOL), bf),
            pltpu.VMEM((2, 2, 128, HALF), fl),
            pltpu.VMEM((2, 2, 3, 8, HALF), fl),
            pltpu.VMEM((2, 8, HALF), fl),
            pltpu.VMEM((2, HALF, 128), fl),
            pltpu.VMEM((CAP, 128), fl),
            pltpu.VMEM((CAP, 128), fl),
            pltpu.VMEM((CAP, 128), jnp.int32),
            pltpu.VMEM((CAP,), jnp.int32),
            pltpu.VMEM((QW,), fl),
            pltpu.VMEM((128,), fl),
            pltpu.VMEM((TCOL,), fl),
            pltpu.SemaphoreType.DMA((SEM_N,)),
            pltpu.SemaphoreType.DMA((SEM_N,)),
            pltpu.SemaphoreType.DMA((9,)),
        ],
        compiler_params=pltpu.CompilerParams(
            collective_id=0, has_side_effects=True, vmem_limit_bytes=60 * 1024 * 1024
        ),
    )(
        tokens,
        w_query,
        w_key,
        w_value,
        w_out.T,
        first_row,
        query_gain,
        key_gain,
        out_gain,
        live_rows,
    )


def solution(mesh):
    in_specs = (
        P("fsdp", "tensor"),
        P("fsdp"),
        P("fsdp"),
        P("fsdp", "tensor"),
        P("fsdp", "tensor"),
        P("fsdp", "tensor"),
        P("tensor", "fsdp"),
        P("tensor"),
        P("tensor"),
        P("tensor"),
    )
    return jax.shard_map(
        body, mesh=mesh, in_specs=in_specs, out_specs=P("fsdp", "tensor"), check_vma=False
    )
```

```python
import functools
import math

import jax
import jax.numpy as jnp
from jax import lax
from jax.experimental import pallas as pl
from jax.experimental.pallas import tpu as pltpu
from jax.sharding import PartitionSpec as P

D = 5120
HEADS = 20
KV_HEADS = 4
HEAD_DIM = 128
CAP = 768
HALF = 384
EPS = 1e-06
ROPE_BASE = 500000.0
SHARD = 160
QKV = 896
QW = 640
TCOL = 1280
MESH = pl.DeviceIdType.MESH

BLOCKS = 2

TOK_CHUNK = 96
TOK_N = CAP // TOK_CHUNK
ATT_CHUNK = 128
ATT_N = CAP // ATT_CHUNK

AG_SEMS = 2 * 24 + 2
SEM_W = 0
SEM_O = SEM_W + AG_SEMS
SEM_T = SEM_O + AG_SEMS
SEM_A = SEM_T + 4 * TOK_N
SEM_S = SEM_A + 4 * ATT_N
SEM_P = SEM_S + 12
SEM_N = SEM_P + 1


def plan(events, rate=45.0, hop=1.8, report=None):
    now, done, arrive, free, order = 0.0, set(), {}, {}, []
    left = list(events)
    while left:
        best = None
        for n, (name, after, waits, sends, cost, late, work) in enumerate(left):
            if any(a not in done for a in after) or any(i not in arrive for i, _ in waits):
                continue
            ready = max([now] + [arrive[i] for i, _ in waits])
            key = (ready, late, n)
            if best is None or key < best[0]:
                best = (key, n)
        (ready, _, _), n = best
        name, after, waits, sends, cost, late, work = left.pop(n)
        now = ready + cost + 0.02
        for idx, link, kb, _ in sends:
            lines = {"yp": ("y+", "y-"), "far": ()}.get(link, (link,))
            begin = max([now] + [free.get(line, 0.0) for line in lines])
            if link == "far" and kb < 100:
                begin = max(now, min(free.get("y+", 0.0), free.get("y-", 0.0)))
            if link == "c":
                busy = finish = begin + kb / 200.0
            else:
                finish = begin + kb / rate
                busy = max(finish, begin + kb / (2 * rate) + hop)
            for line in lines:
                free[line] = busy
            arrive[idx] = finish + (1.0 if link == "c" else 2 * hop if link == "far" else hop)
        done.add(name)
        order.append(name)
        if report is not None:
            report.append((name, now))
    return order


def kernel(
    tok_hbm,
    wq_hbm,
    wk_hbm,
    wv_hbm,
    wot_hbm,
    first_hbm,
    qgain_hbm,
    kgain_hbm,
    ogain_hbm,
    live_ref,
    out_hbm,
    wbuf,
    obuf,
    xall,
    xstage,
    acc,
    rot,
    vbuf,
    att,
    astage,
    oacc,
    res,
    sqt,
    sqr,
    krow,
    qcol,
    cos_ref,
    sin_ref,
    start_ref,
    first_v,
    qgain_v,
    kgain_v,
    ogain_v,
    send_sem,
    recv_sem,
    local_sem,
):
    f = lax.axis_index("fsdp")
    t = lax.axis_index("tensor")
    x, yl, z = f // 8, (f // 4) % 2, f % 4
    yh, core = t // 2, t % 2
    y = 2 * yh + yl

    def dev(dx=0, dy=0, dz=0, flip=0):
        ny = (y + dy) % 4
        nf = ((x + dx) % 4) * 8 + (ny % 2) * 4 + (z + dz) % 4
        nc = (core + flip) % 2
        return (nf, (ny // 2) * 2 + nc)

    ypair = ((x * 8 + (1 - yl) * 4 + z), t)
    swap_f = t * 8 + yl * 4 + z
    swap = (swap_f, x)
    sends = []

    def send(src, dst, idx, to):
        copy = pltpu.make_async_remote_copy(
            src_ref=src,
            dst_ref=dst,
            send_sem=send_sem.at[idx],
            recv_sem=recv_sem.at[idx],
            device_id=to,
            device_id_type=MESH,
        )
        copy.start()
        sends.append(copy)

    def recv(dst, idx):
        pltpu.make_async_remote_copy(
            src_ref=dst,
            dst_ref=dst,
            send_sem=send_sem.at[idx],
            recv_sem=recv_sem.at[idx],
            device_id=ypair,
            device_id_type=MESH,
        ).wait_recv()

    events = []

    def event(name, after=(), waits=(), sends=(), cost=0.0, late=0, work=None):
        events.append((name, tuple(after), tuple(waits), tuple(sends), cost, late, work))

    def run():
        for name in plan(events):
            _, _, waits, outs, _, _, work = next(e for e in events if e[0] == name)
            for idx, dst in waits:
                recv(dst(), idx)
            if work is not None:
                work()
            for idx, _, _, what in outs:
                what(idx)

    written = [
        pltpu.make_async_copy(
            res.at[pl.ds(p * HALF, HALF)], out_hbm.at[pl.ds(p * HALF, HALF)], local_sem.at[p]
        )
        for p in range(2)
    ]

    local = [
        pltpu.make_async_copy(wq_hbm, wbuf.at[x, yl, z, :, pl.ds(0, QW)], local_sem.at[0]),
        pltpu.make_async_copy(wk_hbm, wbuf.at[x, yl, z, :, pl.ds(QW, 128)], local_sem.at[1]),
        pltpu.make_async_copy(wv_hbm, wbuf.at[x, yl, z, :, pl.ds(QW + 128, 128)], local_sem.at[2]),
        pltpu.make_async_copy(tok_hbm, xall.at[t], local_sem.at[3]),
        pltpu.make_async_copy(first_hbm, first_v, local_sem.at[5]),
        pltpu.make_async_copy(qgain_hbm, qgain_v, local_sem.at[6]),
        pltpu.make_async_copy(kgain_hbm, kgain_v, local_sem.at[7]),
        pltpu.make_async_copy(ogain_hbm, ogain_v, local_sem.at[8]),
    ]
    for copy in local:
        copy.start()

    barrier = pltpu.get_barrier_semaphore()
    partners = [
        dev(dx=1), dev(dx=3), dev(dz=1), dev(dz=3), dev(dy=1), dev(dy=3),
        dev(flip=1), dev(dy=2), dev(dy=2, flip=1),
    ]
    for to in partners:
        pl.semaphore_signal(barrier, inc=1, device_id=to, device_id_type=MESH)

    @pl.when(x != t)
    def _():
        pl.semaphore_signal(barrier, inc=1, device_id=swap, device_id_type=MESH)

    pl.semaphore_wait(barrier, len(partners) + jnp.where(x != t, 1, 0))

    def gather(tag, buf, base, kb, start, start_y, paired):
        order = (0, 3, 1, 2)

        def slot(color, da, yy, db):
            dx, dz = (da, db) if color == 0 else (db, da)
            return buf.at[(x + dx) % 4, yy, (z + dz) % 4, pl.ds(color * 80, 80)]

        def pair(color, da, db):
            dx, dz = (da, db) if color == 0 else (db, da)
            return buf.at[(x + dx) % 4, :, (z + dz) % 4, pl.ds(color * 80, 80)]

        def out(color, stage, sign, k, ref, units=1):
            along_x = (stage == 0) == (color == 0)
            d = sign % 4
            to = dev(dx=d) if along_x else dev(dz=d)
            link = ("x" if along_x else "z") + ("+" if sign > 0 else "-")
            return (base + 24 * color + k, link, units * kb, lambda idx: send(ref(), ref(), idx, to))

        def second(c, k):
            da = order[k]
            return [
                out(c, 1, 1, 6 + 4 * k, lambda: pair(c, da, 0), 2),
                out(c, 1, -1, 7 + 4 * k, lambda: pair(c, da, 0), 2),
            ]

        def half(c, yy):
            return buf.at[x, yy, z, pl.ds(c * 80, 80)]

        for c in range(2):
            event(
                f"{tag}y{c}", start_y,
                sends=[(base + 48 + c, "yp", kb, lambda idx, c=c: send(half(c, yl), half(c, yl), idx, ypair))],
            )
        for stage in range(2):
            for c in range(2):
                k = 0 if stage == 0 else 6
                own = functools.partial(half, c, yl)
                if not paired:
                    event(
                        f"{tag}0{stage}{c}", start,
                        sends=[out(c, stage, 1, k, own), out(c, stage, -1, k + 1, own)],
                    )
        for c in range(2):
            sem = base + 24 * c
            other = functools.partial(half, c, 1 - yl)
            both = functools.partial(pair, c, 0, 0)
            if paired:
                first = [out(c, 0, 1, 0, both, 2), out(c, 0, -1, 1, both, 2)] + second(c, 0)
                left0 = [(sem, lambda c=c: pair(c, 3, 0))]
                right0 = [(sem + 1, lambda c=c: pair(c, 1, 0))]
            else:
                first = [
                    out(c, 0, 1, 2, other), out(c, 0, -1, 3, other),
                    out(c, 1, 1, 22, other), out(c, 1, -1, 23, other),
                ]
                left0 = [(sem, lambda c=c: slot(c, 3, yl, 0)), (sem + 2, lambda c=c: slot(c, 3, 1 - yl, 0))]
                right0 = [(sem + 1, lambda c=c: slot(c, 1, yl, 0)), (sem + 3, lambda c=c: slot(c, 1, 1 - yl, 0))]
            event(f"{tag}1{c}", start, waits=[(base + 48 + c, other)], sends=first)
            event(
                f"{tag}2l{c}", waits=left0,
                sends=[out(c, 0, 1, 4, lambda c=c: slot(c, 3, 0, 0))] + second(c, 1),
            )
            event(
                f"{tag}2r{c}", waits=right0,
                sends=[out(c, 0, -1, 5, lambda c=c: slot(c, 1, 1, 0))] + second(c, 2),
            )
            event(
                f"{tag}3{c}",
                waits=[(sem + 4, lambda c=c: slot(c, 2, 0, 0)), (sem + 5, lambda c=c: slot(c, 2, 1, 0))],
                sends=second(c, 3),
            )
            for k in range(4):
                da = order[k]
                near_l = functools.partial(pair, c, da, 3)
                near_r = functools.partial(pair, c, da, 1)
                far = functools.partial(pair, c, da, 2)
                left = [(sem + 6 + 4 * k, near_l)]
                right = [(sem + 7 + 4 * k, near_r)]
                if k == 0 and not paired:
                    left = [
                        (sem + 6, lambda c=c: slot(c, 0, yl, 3)), (sem + 22, lambda c=c: slot(c, 0, 1 - yl, 3)),
                    ]
                    right = [
                        (sem + 7, lambda c=c: slot(c, 0, yl, 1)), (sem + 23, lambda c=c: slot(c, 0, 1 - yl, 1)),
                    ]
                on_l = [out(c, 1, 1, 8 + 4 * k, lambda c=c, da=da: slot(c, da, 0, 3))]
                on_r = [out(c, 1, -1, 9 + 4 * k, lambda c=c, da=da: slot(c, da, 1, 1))]
                end = [
                    (sem + 8 + 4 * k, lambda c=c, da=da: slot(c, da, 0, 2)),
                    (sem + 9 + 4 * k, lambda c=c, da=da: slot(c, da, 1, 2)),
                ]
                if k == 0:
                    on_l, on_r, end = [out(c, 1, 1, 8, near_l, 2)], [], [(sem + 8, far)]
                if k == 1:
                    on_l, on_r, end = [], [out(c, 1, -1, 13, near_r, 2)], [(sem + 13, far)]
                event(f"{tag}4l{c}{k}", waits=left, sends=on_l)
                event(f"{tag}4r{c}{k}", waits=right, sends=on_r)
                event(f"{tag}5{c}{k}", waits=end)

    def plane(tag, dx):
        k = (0, 3, 1, 2).index(dx)
        need = [f"{tag}4l0{k}", f"{tag}4r0{k}", f"{tag}50{k}", f"{tag}2l0", f"{tag}2r0", f"{tag}30"]
        if dx == 0:
            need += [f"{tag}11", f"{tag}2l1", f"{tag}2r1", f"{tag}31"]
        else:
            need += [f"{tag}" + {3: "4l1", 1: "4r1", 2: "51"}[dx] + f"{n}" for n in range(4)]
        return need + [f"{tag}10", f"{tag}11"]

    def spread(tag, buf, stage, base, chunk, i, kb, after, src=None):
        rows = pl.ds(i * chunk, chunk)
        held = stage.at[i % 2, pl.ds((i // 2) * chunk, chunk)]
        own = buf.at[t, rows] if src is None else src.at[rows]
        d, back, link = (1, 3, "y+") if i % 2 == 0 else (3, 1, "y-")
        came = (((y + back) % 4) // 2) * 2 + core
        far = (t + 2) % 4
        sib = (core + 1) % 2
        base = base + 4 * i
        event(
            f"{tag}o{i}", after,
            sends=[
                (base, link, kb, lambda idx: send(own, held, idx, dev(dy=d))),
                (base + 1, "c", kb, lambda idx: send(own, buf.at[t, rows], idx, dev(flip=1))),
            ],
        )
        event(
            f"{tag}r{i}", waits=[(base, lambda: held)],
            sends=[(base + 2, link, kb, lambda idx: send(held, buf.at[came, rows], idx, dev(dy=d)))],
        )
        event(
            f"{tag}i{i}", waits=[(base + 2, lambda: buf.at[far, rows])],
            sends=[(base + 3, "c", kb, lambda idx: send(buf.at[far, rows], buf.at[far, rows], idx, dev(flip=1)))],
        )
        event(
            f"{tag}d{i}",
            waits=[
                (base + 1, lambda: buf.at[yh * 2 + sib, rows]),
                (base + 3, lambda: buf.at[(1 - yh) * 2 + sib, rows]),
            ],
        )

    def exchange(k, p, after):
        cols = pl.ds(p * HALF, HALF)
        outs = []
        for n, to in enumerate((dev(flip=1), dev(dy=2), dev(dy=2, flip=1))):
            outs.append((
                SEM_S + 6 * k + 3 * p + n, "c" if n == 0 else "far", 12,
                lambda idx, n=n, to=to: send(sqt.at[k, p, pl.ds(0, 8)], sqr.at[k, p, n], idx, to),
            ))
        event(f"x{k}{p}", after, sends=outs)

    def exchanged(k, p):
        return [(SEM_S + 6 * k + 3 * p + n, lambda n=n: sqr.at[k, p, n]) for n in range(3)]

    def total(k, p):
        return sqt[k, p, pl.ds(0, 8)] + sqr[k, p, 0] + sqr[k, p, 1] + sqr[k, p, 2]

    def qkv(row, size, dx, first):
        j = (x + dx) % 4
        rows = pl.ds(row, size)
        part = jnp.dot(
            xall[j, rows], wbuf[j].reshape(TCOL, QKV), preferred_element_type=jnp.float32
        )
        if first:
            acc[rows] = part
        else:
            acc[rows] += part

    lane = lax.broadcasted_iota(jnp.int32, (HALF, 128), 1)

    def sums(p):
        rows = pl.ds(p * HALF, HALF)
        q = acc[rows, pl.ds(0, QW)]
        k = acc[rows, pl.ds(QW, 128)]
        qs = jnp.sum(q * q, axis=1, keepdims=True)
        ks = jnp.sum(k * k, axis=1, keepdims=True)
        both = jnp.where(lane < 4, qs, ks)
        sqt[0, p] = both.T

    def tables():
        for copy in local[4:]:
            copy.wait()
        first = jnp.broadcast_to(first_v[...].reshape(1, CAP), (128, CAP)).astype(jnp.float32).T
        wide = lax.broadcasted_iota(jnp.int32, (CAP, 128), 1)
        local_row = lax.broadcasted_iota(jnp.int32, (CAP, 128), 0).astype(jnp.float32)
        freqs = jnp.power(ROPE_BASE, -((wide % 64).astype(jnp.float32) * 2.0 / HEAD_DIM))
        angle = (local_row - first) * freqs
        sine = jnp.sin(angle)
        cos_ref[...] = jnp.cos(angle)
        sin_ref[...] = jnp.where(wide < 64, -sine, sine)
        start_ref[...] = first.astype(jnp.int32)

    def rotate(p):
        rows = pl.ds(p * HALF, HALF)
        gains = jnp.concatenate([qgain_v[...].reshape(1, QW), kgain_v[...].reshape(1, 128)], axis=1)
        for h in range(6):
            cols = pl.ds(h * 128, 128)
            u = acc[rows, cols] * gains[:, h * 128 : (h + 1) * 128]
            r = u * cos_ref[rows] + pltpu.roll(u, 64, 1) * sin_ref[rows]
            rot[h, rows] = r.astype(jnp.bfloat16)
        vbuf[rows] = acc[rows, pl.ds(QW + 128, 128)].astype(jnp.bfloat16)

    def scales(p):
        sq = total(0, p)
        res_q = lax.rsqrt(sq[0:4] / (HEADS * HEAD_DIM) + EPS) * (1.0 / math.sqrt(HEAD_DIM))
        res_k = lax.rsqrt(sq[4:8] / (KV_HEADS * HEAD_DIM) + EPS)
        both = jnp.concatenate([res_q, res_k], axis=0)
        krow[p] = both
        qcol[p] = jnp.concatenate([both] * 16, axis=0).T

    def attend(p, b):
        rows = pl.ds(p * HALF + b * 128, 128)
        width = (b + 1) * 128
        seen = pl.ds(p * HALF, width)
        first = start_ref[rows, 0:1] - p * HALF
        col = lax.broadcasted_iota(jnp.int32, (128, width), 1)
        row = lax.broadcasted_iota(jnp.int32, (128, width), 0) + b * 128
        bias = jnp.where((col >= first) & (col <= row), 0.0, -1e30).astype(jnp.float32)
        scale = qcol[p, pl.ds(b * 128, 128), 0:1] * krow[p, 4:5, 0:width]
        s = lax.dot_general(
            rot[0:5, rows].reshape(QW, 128), rot[5, seen], (((1,), (1,)), ((), ())),
            preferred_element_type=jnp.float32,
        ).reshape(5, 128, width)
        s = s * scale[None] + bias[None]
        e = jnp.exp(s - jnp.max(s, axis=2, keepdims=True))
        inv = 1.0 / jnp.sum(e, axis=2, keepdims=True)
        o = jnp.dot(
            e.astype(jnp.bfloat16).reshape(QW, width), vbuf[seen], preferred_element_type=jnp.float32
        ).reshape(5, 128, 128)
        o = (o * inv).astype(jnp.bfloat16)
        for h in range(5):
            att[t, rows, pl.ds(h * 128, 128)] = o[h]

    def project(p, dx, first):
        j = (x + dx) % 4
        rows = pl.ds(p * HALF, HALF)
        part = lax.dot_general(
            att[j, rows],
            obuf[j].reshape(TCOL, QW),
            (((1,), (1,)), ((), ())),
            preferred_element_type=jnp.float32,
        )
        if first:
            oacc[rows] = part
        else:
            oacc[rows] += part

    def out_sums(p):
        rows = pl.ds(p * HALF, HALF)
        o = oacc[rows]
        sqt[1, p] = jnp.broadcast_to(jnp.sum(o * o, axis=1, keepdims=True), (HALF, 128)).T

    def finish(p):
        sums_out = jnp.concatenate([total(1, p)] * 16, axis=0).T
        rows = pl.ds(p * HALF, HALF)
        scale = lax.rsqrt(sums_out[:, 0:1] / D + EPS)
        r = xall[t, rows].astype(jnp.float32) + oacc[rows] * scale * ogain_v[...].reshape(1, TCOL)
        row = lax.broadcasted_iota(jnp.int32, (HALF, TCOL), 0) + p * HALF
        res[rows] = jnp.where(row < live_ref[0], r, 0.0).astype(jnp.bfloat16)
        written[p].start()

    for copy in local[:3]:
        copy.wait()

    own_o = obuf.at[x, yl, z]

    def swap_out():
        @pl.when(x != t)
        def _():
            copy = pltpu.make_async_remote_copy(
                src_ref=wot_hbm, dst_ref=obuf.at[t, yl, z], send_sem=send_sem.at[SEM_P],
                recv_sem=recv_sem.at[SEM_P], device_id=swap, device_id_type=MESH,
            )
            copy.start()

        @pl.when(x == t)
        def _():
            copy = pltpu.make_async_copy(wot_hbm, own_o, local_sem.at[4])
            copy.start()

    def swap_in():
        @pl.when(x != t)
        def _():
            copy = pltpu.make_async_remote_copy(
                src_ref=wot_hbm, dst_ref=own_o, send_sem=send_sem.at[SEM_P],
                recv_sem=recv_sem.at[SEM_P], device_id=swap, device_id_type=MESH,
            )
            copy.wait()

        @pl.when(x == t)
        def _():
            copy = pltpu.make_async_copy(wot_hbm, own_o, local_sem.at[4])
            copy.wait()

    w_sends = [f"w4{s}{c}{k}" for s in "lr" for c in range(2) for k in range(4)]
    gather("w", wbuf, SEM_W, 143.4, (), (), False)
    event("swap", ("w010", "w011"), sends=[(SEM_P, "far", 205, lambda idx: swap_out())])
    for i in range(TOK_N):
        spread("t", xall, xstage, SEM_T, TOK_CHUNK, i, 245.8, ("wy0", "wy1", "w010", "w011"), tok_hbm)
    event("swapped", ("swap", "tr3"), cost=0.1, work=swap_in)
    gather("o", obuf, SEM_O, 102.4, ["swapped"] + w_sends, ["swapped", "tr7"], False)
    event("own", work=local[3].wait)
    event("tables", ["to7"], cost=3.0, late=1, work=tables)

    for p in range(2):
        blocks = [(0, HALF)] if p == 0 else [(HALF, HALF // 2), (HALF + HALF // 2, HALF // 2)]
        for m, (row, size) in enumerate(blocks):
            chunks = range(row // TOK_CHUNK, (row + size) // TOK_CHUNK)
            rows_in = ["own"] + [f"t{s}{i}" for s in "rid" for i in chunks]
            for n, dx in enumerate((0, 3, 1, 2)):
                event(
                    f"q{p}{m}{n}", rows_in + plane("w", dx) + ([f"q{p}{m}{n - 1}"] if n else []),
                    cost=1.25 * size / HALF, late=1, work=functools.partial(qkv, row, size, dx, n == 0),
                )
        event(f"sum{p}", [f"q{p}{m}3" for m in range(len(blocks))], cost=0.2, late=1, work=functools.partial(sums, p))
        exchange(0, p, [f"sum{p}"])
        event(f"rot{p}", [f"x0{p}", "tables"], cost=0.4, late=1, work=functools.partial(rotate, p))
        event(f"scale{p}", [f"rot{p}"], waits=exchanged(0, p), cost=0.2, late=1, work=functools.partial(scales, p))
    half_a = ATT_N // 2
    for i in range(ATT_N):
        p, b = i // 3, i % 3
        prev = f"att{i - 1}" if b else f"scale{p}"
        event(f"att{i}", (prev,), cost=0.6 + 0.4 * b, late=0.5 + p, work=functools.partial(attend, p, b))
        spread("a", att, astage, SEM_A, ATT_CHUNK, i, 163.8, (f"att{i}",))
    for p in range(2):
        rows_in = [f"a{s}{p * half_a + i}" for s in "orid" for i in range(half_a)]
        for n, dx in enumerate((0, 3, 1, 2)):
            event(
                f"p{p}{n}", rows_in + plane("o", dx) + ([f"p{p}{n - 1}"] if n else []),
                cost=0.7, late=1, work=functools.partial(project, p, dx, n == 0),
            )
        event(f"osum{p}", [f"p{p}3"], cost=0.2, late=1, work=functools.partial(out_sums, p))
        exchange(1, p, [f"osum{p}"])
        event(f"end{p}", (f"x1{p}",), waits=exchanged(1, p), cost=1.2, late=1, work=functools.partial(finish, p))
    run()
    for copy in written:
        copy.wait()
    for copy in sends:
        copy.wait_send()


def put_out(src, dst):
    dst[...] = src[...]


def body(
    tokens, live_rows, first_row, w_query, w_key, w_value, w_out, query_gain, key_gain, out_gain
):
    hbm = pl.BlockSpec(memory_space=pltpu.HBM)
    smem = pl.BlockSpec(memory_space=pltpu.SMEM)
    bf, fl = jnp.bfloat16, jnp.float32
    result = pl.pallas_call(
        kernel,
        out_shape=jax.ShapeDtypeStruct((CAP, TCOL), bf),
        in_specs=[hbm] * 9 + [smem],
        out_specs=pl.BlockSpec(memory_space=pl.ANY),
        scratch_shapes=[
            pltpu.VMEM((4, 2, 4, SHARD, QKV), bf),
            pltpu.VMEM((4, 2, 4, SHARD, QW), bf),
            pltpu.VMEM((4, CAP, TCOL), bf),
            pltpu.VMEM((2, HALF, TCOL), bf),
            pltpu.VMEM((CAP, QKV), fl),
            pltpu.VMEM((6, CAP, 128), bf),
            pltpu.VMEM((CAP, 128), bf),
            pltpu.VMEM((4, CAP, QW), bf),
            pltpu.VMEM((2, HALF, QW), bf),
            pltpu.VMEM((CAP, TCOL), fl),
            pltpu.VMEM((CAP, TCOL), bf),
            pltpu.VMEM((2, 2, 128, HALF), fl),
            pltpu.VMEM((2, 2, 3, 8, HALF), fl),
            pltpu.VMEM((2, 8, HALF), fl),
            pltpu.VMEM((2, HALF, 128), fl),
            pltpu.VMEM((CAP, 128), fl),
            pltpu.VMEM((CAP, 128), fl),
            pltpu.VMEM((CAP, 128), jnp.int32),
            pltpu.VMEM((CAP,), jnp.int32),
            pltpu.VMEM((QW,), fl),
            pltpu.VMEM((128,), fl),
            pltpu.VMEM((TCOL,), fl),
            pltpu.SemaphoreType.DMA((SEM_N,)),
            pltpu.SemaphoreType.DMA((SEM_N,)),
            pltpu.SemaphoreType.DMA((9,)),
        ],
        compiler_params=pltpu.CompilerParams(
            collective_id=0, has_side_effects=True, vmem_limit_bytes=60 * 1024 * 1024
        ),
    )(
        tokens,
        w_query,
        w_key,
        w_value,
        w_out.T,
        first_row,
        query_gain,
        key_gain,
        out_gain,
        live_rows,
    )
    block = pl.BlockSpec((CAP // BLOCKS, TCOL), lambda i: (i, 0))
    return pl.pallas_call(
        put_out,
        grid=(BLOCKS,),
        out_shape=jax.ShapeDtypeStruct((CAP, TCOL), bf),
        in_specs=[block],
        out_specs=block,
    )(result)


def solution(mesh):
    in_specs = (
        P("fsdp", "tensor"),
        P("fsdp"),
        P("fsdp"),
        P("fsdp", "tensor"),
        P("fsdp", "tensor"),
        P("fsdp", "tensor"),
        P("tensor", "fsdp"),
        P("tensor"),
        P("tensor"),
        P("tensor"),
    )
    return jax.shard_map(
        body, mesh=mesh, in_specs=in_specs, out_specs=P("fsdp", "tensor"), check_vma=False
    )
```

```python
import functools
import math

import jax
import jax.numpy as jnp
from jax import lax
from jax.experimental import pallas as pl
from jax.experimental.pallas import tpu as pltpu
from jax.sharding import PartitionSpec as P

D = 5120
HEADS = 20
KV_HEADS = 4
HEAD_DIM = 128
CAP = 768
HALF = 384
EPS = 1e-06
ROPE_BASE = 500000.0
SHARD = 160
QKV = 896
QW = 640
TCOL = 1280
MESH = pl.DeviceIdType.MESH

BLOCKS = 3

TOK_CHUNK = 96
TOK_N = CAP // TOK_CHUNK
ATT_CHUNK = 128
ATT_N = CAP // ATT_CHUNK

AG_SEMS = 2 * 24 + 2
SEM_W = 0
SEM_O = SEM_W + AG_SEMS
SEM_T = SEM_O + AG_SEMS
SEM_A = SEM_T + 4 * TOK_N
SEM_S = SEM_A + 4 * ATT_N
SEM_P = SEM_S + 12
SEM_N = SEM_P + 1


def plan(events, rate=45.0, hop=1.8, report=None):
    now, done, arrive, free, order = 0.0, set(), {}, {}, []
    left = list(events)
    while left:
        best = None
        for n, (name, after, waits, sends, cost, late, work) in enumerate(left):
            if any(a not in done for a in after) or any(i not in arrive for i, _ in waits):
                continue
            ready = max([now] + [arrive[i] for i, _ in waits])
            key = (ready, late, n)
            if best is None or key < best[0]:
                best = (key, n)
        (ready, _, _), n = best
        name, after, waits, sends, cost, late, work = left.pop(n)
        now = ready + cost + 0.02
        for idx, link, kb, _ in sends:
            lines = {"yp": ("y+", "y-"), "far": ()}.get(link, (link,))
            begin = max([now] + [free.get(line, 0.0) for line in lines])
            if link == "far" and kb < 100:
                begin = max(now, min(free.get("y+", 0.0), free.get("y-", 0.0)))
            if link == "c":
                busy = finish = begin + kb / 200.0
            else:
                finish = begin + kb / rate
                busy = max(finish, begin + kb / (2 * rate) + hop)
            for line in lines:
                free[line] = busy
            arrive[idx] = finish + (1.0 if link == "c" else 2 * hop if link == "far" else hop)
        done.add(name)
        order.append(name)
        if report is not None:
            report.append((name, now))
    return order


def kernel(
    tok_hbm,
    wq_hbm,
    wk_hbm,
    wv_hbm,
    wot_hbm,
    first_hbm,
    qgain_hbm,
    kgain_hbm,
    ogain_hbm,
    live_ref,
    out_hbm,
    wbuf,
    obuf,
    xall,
    xstage,
    acc,
    rot,
    vbuf,
    att,
    astage,
    oacc,
    res,
    sqt,
    sqr,
    krow,
    qcol,
    cos_ref,
    sin_ref,
    start_ref,
    first_v,
    qgain_v,
    kgain_v,
    ogain_v,
    send_sem,
    recv_sem,
    local_sem,
):
    f = lax.axis_index("fsdp")
    t = lax.axis_index("tensor")
    x, yl, z = f // 8, (f // 4) % 2, f % 4
    yh, core = t // 2, t % 2
    y = 2 * yh + yl

    def dev(dx=0, dy=0, dz=0, flip=0):
        ny = (y + dy) % 4
        nf = ((x + dx) % 4) * 8 + (ny % 2) * 4 + (z + dz) % 4
        nc = (core + flip) % 2
        return (nf, (ny // 2) * 2 + nc)

    ypair = ((x * 8 + (1 - yl) * 4 + z), t)
    swap_f = t * 8 + yl * 4 + z
    swap = (swap_f, x)
    sends = []

    def send(src, dst, idx, to):
        copy = pltpu.make_async_remote_copy(
            src_ref=src,
            dst_ref=dst,
            send_sem=send_sem.at[idx],
            recv_sem=recv_sem.at[idx],
            device_id=to,
            device_id_type=MESH,
        )
        copy.start()
        sends.append(copy)

    def recv(dst, idx):
        pltpu.make_async_remote_copy(
            src_ref=dst,
            dst_ref=dst,
            send_sem=send_sem.at[idx],
            recv_sem=recv_sem.at[idx],
            device_id=ypair,
            device_id_type=MESH,
        ).wait_recv()

    events = []

    def event(name, after=(), waits=(), sends=(), cost=0.0, late=0, work=None):
        events.append((name, tuple(after), tuple(waits), tuple(sends), cost, late, work))

    def run():
        for name in plan(events):
            _, _, waits, outs, _, _, work = next(e for e in events if e[0] == name)
            for idx, dst in waits:
                recv(dst(), idx)
            if work is not None:
                work()
            for idx, _, _, what in outs:
                what(idx)

    written = [
        pltpu.make_async_copy(
            res.at[pl.ds(p * HALF, HALF)], out_hbm.at[pl.ds(p * HALF, HALF)], local_sem.at[p]
        )
        for p in range(2)
    ]

    local = [
        pltpu.make_async_copy(wq_hbm, wbuf.at[x, yl, z, :, pl.ds(0, QW)], local_sem.at[0]),
        pltpu.make_async_copy(wk_hbm, wbuf.at[x, yl, z, :, pl.ds(QW, 128)], local_sem.at[1]),
        pltpu.make_async_copy(wv_hbm, wbuf.at[x, yl, z, :, pl.ds(QW + 128, 128)], local_sem.at[2]),
        pltpu.make_async_copy(tok_hbm, xall.at[t], local_sem.at[3]),
        pltpu.make_async_copy(first_hbm, first_v, local_sem.at[5]),
        pltpu.make_async_copy(qgain_hbm, qgain_v, local_sem.at[6]),
        pltpu.make_async_copy(kgain_hbm, kgain_v, local_sem.at[7]),
        pltpu.make_async_copy(ogain_hbm, ogain_v, local_sem.at[8]),
    ]
    for copy in local:
        copy.start()

    barrier = pltpu.get_barrier_semaphore()
    partners = [
        dev(dx=1), dev(dx=3), dev(dz=1), dev(dz=3), dev(dy=1), dev(dy=3),
        dev(flip=1), dev(dy=2), dev(dy=2, flip=1),
    ]
    for to in partners:
        pl.semaphore_signal(barrier, inc=1, device_id=to, device_id_type=MESH)

    @pl.when(x != t)
    def _():
        pl.semaphore_signal(barrier, inc=1, device_id=swap, device_id_type=MESH)

    pl.semaphore_wait(barrier, len(partners) + jnp.where(x != t, 1, 0))

    def gather(tag, buf, base, kb, start, start_y, paired):
        order = (0, 3, 1, 2)

        def slot(color, da, yy, db):
            dx, dz = (da, db) if color == 0 else (db, da)
            return buf.at[(x + dx) % 4, yy, (z + dz) % 4, pl.ds(color * 80, 80)]

        def pair(color, da, db):
            dx, dz = (da, db) if color == 0 else (db, da)
            return buf.at[(x + dx) % 4, :, (z + dz) % 4, pl.ds(color * 80, 80)]

        def out(color, stage, sign, k, ref, units=1):
            along_x = (stage == 0) == (color == 0)
            d = sign % 4
            to = dev(dx=d) if along_x else dev(dz=d)
            link = ("x" if along_x else "z") + ("+" if sign > 0 else "-")
            return (base + 24 * color + k, link, units * kb, lambda idx: send(ref(), ref(), idx, to))

        def second(c, k):
            da = order[k]
            return [
                out(c, 1, 1, 6 + 4 * k, lambda: pair(c, da, 0), 2),
                out(c, 1, -1, 7 + 4 * k, lambda: pair(c, da, 0), 2),
            ]

        def half(c, yy):
            return buf.at[x, yy, z, pl.ds(c * 80, 80)]

        for c in range(2):
            event(
                f"{tag}y{c}", start_y,
                sends=[(base + 48 + c, "yp", kb, lambda idx, c=c: send(half(c, yl), half(c, yl), idx, ypair))],
            )
        for stage in range(2):
            for c in range(2):
                k = 0 if stage == 0 else 6
                own = functools.partial(half, c, yl)
                if not paired:
                    event(
                        f"{tag}0{stage}{c}", start,
                        sends=[out(c, stage, 1, k, own), out(c, stage, -1, k + 1, own)],
                    )
        for c in range(2):
            sem = base + 24 * c
            other = functools.partial(half, c, 1 - yl)
            both = functools.partial(pair, c, 0, 0)
            if paired:
                first = [out(c, 0, 1, 0, both, 2), out(c, 0, -1, 1, both, 2)] + second(c, 0)
                left0 = [(sem, lambda c=c: pair(c, 3, 0))]
                right0 = [(sem + 1, lambda c=c: pair(c, 1, 0))]
            else:
                first = [
                    out(c, 0, 1, 2, other), out(c, 0, -1, 3, other),
                    out(c, 1, 1, 22, other), out(c, 1, -1, 23, other),
                ]
                left0 = [(sem, lambda c=c: slot(c, 3, yl, 0)), (sem + 2, lambda c=c: slot(c, 3, 1 - yl, 0))]
                right0 = [(sem + 1, lambda c=c: slot(c, 1, yl, 0)), (sem + 3, lambda c=c: slot(c, 1, 1 - yl, 0))]
            event(f"{tag}1{c}", start, waits=[(base + 48 + c, other)], sends=first)
            event(
                f"{tag}2l{c}", waits=left0,
                sends=[out(c, 0, 1, 4, lambda c=c: slot(c, 3, 0, 0))] + second(c, 1),
            )
            event(
                f"{tag}2r{c}", waits=right0,
                sends=[out(c, 0, -1, 5, lambda c=c: slot(c, 1, 1, 0))] + second(c, 2),
            )
            event(
                f"{tag}3{c}",
                waits=[(sem + 4, lambda c=c: slot(c, 2, 0, 0)), (sem + 5, lambda c=c: slot(c, 2, 1, 0))],
                sends=second(c, 3),
            )
            for k in range(4):
                da = order[k]
                near_l = functools.partial(pair, c, da, 3)
                near_r = functools.partial(pair, c, da, 1)
                far = functools.partial(pair, c, da, 2)
                left = [(sem + 6 + 4 * k, near_l)]
                right = [(sem + 7 + 4 * k, near_r)]
                if k == 0 and not paired:
                    left = [
                        (sem + 6, lambda c=c: slot(c, 0, yl, 3)), (sem + 22, lambda c=c: slot(c, 0, 1 - yl, 3)),
                    ]
                    right = [
                        (sem + 7, lambda c=c: slot(c, 0, yl, 1)), (sem + 23, lambda c=c: slot(c, 0, 1 - yl, 1)),
                    ]
                on_l = [out(c, 1, 1, 8 + 4 * k, lambda c=c, da=da: slot(c, da, 0, 3))]
                on_r = [out(c, 1, -1, 9 + 4 * k, lambda c=c, da=da: slot(c, da, 1, 1))]
                end = [
                    (sem + 8 + 4 * k, lambda c=c, da=da: slot(c, da, 0, 2)),
                    (sem + 9 + 4 * k, lambda c=c, da=da: slot(c, da, 1, 2)),
                ]
                if k == 0:
                    on_l, on_r, end = [out(c, 1, 1, 8, near_l, 2)], [], [(sem + 8, far)]
                if k == 1:
                    on_l, on_r, end = [], [out(c, 1, -1, 13, near_r, 2)], [(sem + 13, far)]
                event(f"{tag}4l{c}{k}", waits=left, sends=on_l)
                event(f"{tag}4r{c}{k}", waits=right, sends=on_r)
                event(f"{tag}5{c}{k}", waits=end)

    def plane(tag, dx):
        k = (0, 3, 1, 2).index(dx)
        need = [f"{tag}4l0{k}", f"{tag}4r0{k}", f"{tag}50{k}", f"{tag}2l0", f"{tag}2r0", f"{tag}30"]
        if dx == 0:
            need += [f"{tag}11", f"{tag}2l1", f"{tag}2r1", f"{tag}31"]
        else:
            need += [f"{tag}" + {3: "4l1", 1: "4r1", 2: "51"}[dx] + f"{n}" for n in range(4)]
        return need + [f"{tag}10", f"{tag}11"]

    def spread(tag, buf, stage, base, chunk, i, kb, after, src=None):
        rows = pl.ds(i * chunk, chunk)
        held = stage.at[i % 2, pl.ds((i // 2) * chunk, chunk)]
        own = buf.at[t, rows] if src is None else src.at[rows]
        d, back, link = (1, 3, "y+") if i % 2 == 0 else (3, 1, "y-")
        came = (((y + back) % 4) // 2) * 2 + core
        far = (t + 2) % 4
        sib = (core + 1) % 2
        base = base + 4 * i
        event(
            f"{tag}o{i}", after,
            sends=[
                (base, link, kb, lambda idx: send(own, held, idx, dev(dy=d))),
                (base + 1, "c", kb, lambda idx: send(own, buf.at[t, rows], idx, dev(flip=1))),
            ],
        )
        event(
            f"{tag}r{i}", waits=[(base, lambda: held)],
            sends=[(base + 2, link, kb, lambda idx: send(held, buf.at[came, rows], idx, dev(dy=d)))],
        )
        event(
            f"{tag}i{i}", waits=[(base + 2, lambda: buf.at[far, rows])],
            sends=[(base + 3, "c", kb, lambda idx: send(buf.at[far, rows], buf.at[far, rows], idx, dev(flip=1)))],
        )
        event(
            f"{tag}d{i}",
            waits=[
                (base + 1, lambda: buf.at[yh * 2 + sib, rows]),
                (base + 3, lambda: buf.at[(1 - yh) * 2 + sib, rows]),
            ],
        )

    def exchange(k, p, after):
        cols = pl.ds(p * HALF, HALF)
        outs = []
        for n, to in enumerate((dev(flip=1), dev(dy=2), dev(dy=2, flip=1))):
            outs.append((
                SEM_S + 6 * k + 3 * p + n, "c" if n == 0 else "far", 12,
                lambda idx, n=n, to=to: send(sqt.at[k, p, pl.ds(0, 8)], sqr.at[k, p, n], idx, to),
            ))
        event(f"x{k}{p}", after, sends=outs)

    def exchanged(k, p):
        return [(SEM_S + 6 * k + 3 * p + n, lambda n=n: sqr.at[k, p, n]) for n in range(3)]

    def total(k, p):
        return sqt[k, p, pl.ds(0, 8)] + sqr[k, p, 0] + sqr[k, p, 1] + sqr[k, p, 2]

    def qkv(row, size, dx, first):
        j = (x + dx) % 4
        rows = pl.ds(row, size)
        part = jnp.dot(
            xall[j, rows], wbuf[j].reshape(TCOL, QKV), preferred_element_type=jnp.float32
        )
        if first:
            acc[rows] = part
        else:
            acc[rows] += part

    lane = lax.broadcasted_iota(jnp.int32, (HALF, 128), 1)

    def sums(p):
        rows = pl.ds(p * HALF, HALF)
        q = acc[rows, pl.ds(0, QW)]
        k = acc[rows, pl.ds(QW, 128)]
        qs = jnp.sum(q * q, axis=1, keepdims=True)
        ks = jnp.sum(k * k, axis=1, keepdims=True)
        both = jnp.where(lane < 4, qs, ks)
        sqt[0, p] = both.T

    def tables():
        for copy in local[4:]:
            copy.wait()
        first = jnp.broadcast_to(first_v[...].reshape(1, CAP), (128, CAP)).astype(jnp.float32).T
        wide = lax.broadcasted_iota(jnp.int32, (CAP, 128), 1)
        local_row = lax.broadcasted_iota(jnp.int32, (CAP, 128), 0).astype(jnp.float32)
        freqs = jnp.power(ROPE_BASE, -((wide % 64).astype(jnp.float32) * 2.0 / HEAD_DIM))
        angle = (local_row - first) * freqs
        sine = jnp.sin(angle)
        cos_ref[...] = jnp.cos(angle)
        sin_ref[...] = jnp.where(wide < 64, -sine, sine)
        start_ref[...] = first.astype(jnp.int32)

    def rotate(p):
        rows = pl.ds(p * HALF, HALF)
        gains = jnp.concatenate([qgain_v[...].reshape(1, QW), kgain_v[...].reshape(1, 128)], axis=1)
        for h in range(6):
            cols = pl.ds(h * 128, 128)
            u = acc[rows, cols] * gains[:, h * 128 : (h + 1) * 128]
            r = u * cos_ref[rows] + pltpu.roll(u, 64, 1) * sin_ref[rows]
            rot[h, rows] = r.astype(jnp.bfloat16)
        vbuf[rows] = acc[rows, pl.ds(QW + 128, 128)].astype(jnp.bfloat16)

    def scales(p):
        sq = total(0, p)
        res_q = lax.rsqrt(sq[0:4] / (HEADS * HEAD_DIM) + EPS) * (1.0 / math.sqrt(HEAD_DIM))
        res_k = lax.rsqrt(sq[4:8] / (KV_HEADS * HEAD_DIM) + EPS)
        both = jnp.concatenate([res_q, res_k], axis=0)
        krow[p] = both
        qcol[p] = jnp.concatenate([both] * 16, axis=0).T

    def attend(p, b):
        rows = pl.ds(p * HALF + b * 128, 128)
        width = (b + 1) * 128
        seen = pl.ds(p * HALF, width)
        first = start_ref[rows, 0:1] - p * HALF
        col = lax.broadcasted_iota(jnp.int32, (128, width), 1)
        row = lax.broadcasted_iota(jnp.int32, (128, width), 0) + b * 128
        bias = jnp.where((col >= first) & (col <= row), 0.0, -1e30).astype(jnp.float32)
        scale = qcol[p, pl.ds(b * 128, 128), 0:1] * krow[p, 4:5, 0:width]
        s = lax.dot_general(
            rot[0:5, rows].reshape(QW, 128), rot[5, seen], (((1,), (1,)), ((), ())),
            preferred_element_type=jnp.float32,
        ).reshape(5, 128, width)
        s = s * scale[None] + bias[None]
        e = jnp.exp(s - jnp.max(s, axis=2, keepdims=True))
        inv = 1.0 / jnp.sum(e, axis=2, keepdims=True)
        o = jnp.dot(
            e.astype(jnp.bfloat16).reshape(QW, width), vbuf[seen], preferred_element_type=jnp.float32
        ).reshape(5, 128, 128)
        o = (o * inv).astype(jnp.bfloat16)
        for h in range(5):
            att[t, rows, pl.ds(h * 128, 128)] = o[h]

    def project(p, dx, first):
        j = (x + dx) % 4
        rows = pl.ds(p * HALF, HALF)
        part = lax.dot_general(
            att[j, rows],
            obuf[j].reshape(TCOL, QW),
            (((1,), (1,)), ((), ())),
            preferred_element_type=jnp.float32,
        )
        if first:
            oacc[rows] = part
        else:
            oacc[rows] += part

    def out_sums(p):
        rows = pl.ds(p * HALF, HALF)
        o = oacc[rows]
        sqt[1, p] = jnp.broadcast_to(jnp.sum(o * o, axis=1, keepdims=True), (HALF, 128)).T

    def finish(p):
        sums_out = jnp.concatenate([total(1, p)] * 16, axis=0).T
        rows = pl.ds(p * HALF, HALF)
        scale = lax.rsqrt(sums_out[:, 0:1] / D + EPS)
        r = xall[t, rows].astype(jnp.float32) + oacc[rows] * scale * ogain_v[...].reshape(1, TCOL)
        row = lax.broadcasted_iota(jnp.int32, (HALF, TCOL), 0) + p * HALF
        res[rows] = jnp.where(row < live_ref[0], r, 0.0).astype(jnp.bfloat16)
        written[p].start()

    for copy in local[:3]:
        copy.wait()

    own_o = obuf.at[x, yl, z]

    def swap_out():
        @pl.when(x != t)
        def _():
            copy = pltpu.make_async_remote_copy(
                src_ref=wot_hbm, dst_ref=obuf.at[t, yl, z], send_sem=send_sem.at[SEM_P],
                recv_sem=recv_sem.at[SEM_P], device_id=swap, device_id_type=MESH,
            )
            copy.start()

        @pl.when(x == t)
        def _():
            copy = pltpu.make_async_copy(wot_hbm, own_o, local_sem.at[4])
            copy.start()

    def swap_in():
        @pl.when(x != t)
        def _():
            copy = pltpu.make_async_remote_copy(
                src_ref=wot_hbm, dst_ref=own_o, send_sem=send_sem.at[SEM_P],
                recv_sem=recv_sem.at[SEM_P], device_id=swap, device_id_type=MESH,
            )
            copy.wait()

        @pl.when(x == t)
        def _():
            copy = pltpu.make_async_copy(wot_hbm, own_o, local_sem.at[4])
            copy.wait()

    w_sends = [f"w4{s}{c}{k}" for s in "lr" for c in range(2) for k in range(4)]
    gather("w", wbuf, SEM_W, 143.4, (), (), False)
    event("swap", ("w010", "w011"), sends=[(SEM_P, "far", 205, lambda idx: swap_out())])
    for i in range(TOK_N):
        spread("t", xall, xstage, SEM_T, TOK_CHUNK, i, 245.8, ("wy0", "wy1", "w010", "w011"), tok_hbm)
    event("swapped", ("swap", "tr3"), cost=0.1, work=swap_in)
    gather("o", obuf, SEM_O, 102.4, ["swapped"] + w_sends, ["swapped", "tr7"], False)
    event("own", work=local[3].wait)
    event("tables", ["to7"], cost=3.0, late=1, work=tables)

    for p in range(2):
        blocks = [(0, HALF)] if p == 0 else [(HALF, HALF // 2), (HALF + HALF // 2, HALF // 2)]
        for m, (row, size) in enumerate(blocks):
            chunks = range(row // TOK_CHUNK, (row + size) // TOK_CHUNK)
            rows_in = ["own"] + [f"t{s}{i}" for s in "rid" for i in chunks]
            for n, dx in enumerate((0, 3, 1, 2)):
                event(
                    f"q{p}{m}{n}", rows_in + plane("w", dx) + ([f"q{p}{m}{n - 1}"] if n else []),
                    cost=1.25 * size / HALF, late=1, work=functools.partial(qkv, row, size, dx, n == 0),
                )
        event(f"sum{p}", [f"q{p}{m}3" for m in range(len(blocks))], cost=0.2, late=1, work=functools.partial(sums, p))
        exchange(0, p, [f"sum{p}"])
        event(f"rot{p}", [f"x0{p}", "tables"], cost=0.4, late=1, work=functools.partial(rotate, p))
        event(f"scale{p}", [f"rot{p}"], waits=exchanged(0, p), cost=0.2, late=1, work=functools.partial(scales, p))
    half_a = ATT_N // 2
    for i in range(ATT_N):
        p, b = i // 3, i % 3
        prev = f"att{i - 1}" if b else f"scale{p}"
        event(f"att{i}", (prev,), cost=0.6 + 0.4 * b, late=0.5 + p, work=functools.partial(attend, p, b))
        spread("a", att, astage, SEM_A, ATT_CHUNK, i, 163.8, (f"att{i}",))
    for p in range(2):
        rows_in = [f"a{s}{p * half_a + i}" for s in "orid" for i in range(half_a)]
        for n, dx in enumerate((0, 3, 1, 2)):
            event(
                f"p{p}{n}", rows_in + plane("o", dx) + ([f"p{p}{n - 1}"] if n else []),
                cost=0.7, late=1, work=functools.partial(project, p, dx, n == 0),
            )
        event(f"osum{p}", [f"p{p}3"], cost=0.2, late=1, work=functools.partial(out_sums, p))
        exchange(1, p, [f"osum{p}"])
        event(f"end{p}", (f"x1{p}",), waits=exchanged(1, p), cost=1.2, late=1, work=functools.partial(finish, p))
    run()
    for copy in written:
        copy.wait()
    for copy in sends:
        copy.wait_send()


def put_out(src, dst):
    dst[...] = src[...]


def body(
    tokens, live_rows, first_row, w_query, w_key, w_value, w_out, query_gain, key_gain, out_gain
):
    hbm = pl.BlockSpec(memory_space=pltpu.HBM)
    smem = pl.BlockSpec(memory_space=pltpu.SMEM)
    bf, fl = jnp.bfloat16, jnp.float32
    result = pl.pallas_call(
        kernel,
        out_shape=jax.ShapeDtypeStruct((CAP, TCOL), bf),
        in_specs=[hbm] * 9 + [smem],
        out_specs=pl.BlockSpec(memory_space=pl.ANY),
        scratch_shapes=[
            pltpu.VMEM((4, 2, 4, SHARD, QKV), bf),
            pltpu.VMEM((4, 2, 4, SHARD, QW), bf),
            pltpu.VMEM((4, CAP, TCOL), bf),
            pltpu.VMEM((2, HALF, TCOL), bf),
            pltpu.VMEM((CAP, QKV), fl),
            pltpu.VMEM((6, CAP, 128), bf),
            pltpu.VMEM((CAP, 128), bf),
            pltpu.VMEM((4, CAP, QW), bf),
            pltpu.VMEM((2, HALF, QW), bf),
            pltpu.VMEM((CAP, TCOL), fl),
            pltpu.VMEM((CAP, TCOL), bf),
            pltpu.VMEM((2, 2, 128, HALF), fl),
            pltpu.VMEM((2, 2, 3, 8, HALF), fl),
            pltpu.VMEM((2, 8, HALF), fl),
            pltpu.VMEM((2, HALF, 128), fl),
            pltpu.VMEM((CAP, 128), fl),
            pltpu.VMEM((CAP, 128), fl),
            pltpu.VMEM((CAP, 128), jnp.int32),
            pltpu.VMEM((CAP,), jnp.int32),
            pltpu.VMEM((QW,), fl),
            pltpu.VMEM((128,), fl),
            pltpu.VMEM((TCOL,), fl),
            pltpu.SemaphoreType.DMA((SEM_N,)),
            pltpu.SemaphoreType.DMA((SEM_N,)),
            pltpu.SemaphoreType.DMA((9,)),
        ],
        compiler_params=pltpu.CompilerParams(
            collective_id=0, has_side_effects=True, vmem_limit_bytes=60 * 1024 * 1024
        ),
    )(
        tokens,
        w_query,
        w_key,
        w_value,
        w_out.T,
        first_row,
        query_gain,
        key_gain,
        out_gain,
        live_rows,
    )
    block = pl.BlockSpec((CAP // BLOCKS, TCOL), lambda i: (i, 0))
    return pl.pallas_call(
        put_out,
        grid=(BLOCKS,),
        out_shape=jax.ShapeDtypeStruct((CAP, TCOL), bf),
        in_specs=[block],
        out_specs=block,
    )(result)


def solution(mesh):
    in_specs = (
        P("fsdp", "tensor"),
        P("fsdp"),
        P("fsdp"),
        P("fsdp", "tensor"),
        P("fsdp", "tensor"),
        P("fsdp", "tensor"),
        P("tensor", "fsdp"),
        P("tensor"),
        P("tensor"),
        P("tensor"),
    )
    return jax.shard_map(
        body, mesh=mesh, in_specs=in_specs, out_specs=P("fsdp", "tensor"), check_vma=False
    )
```
